32 devices in a mesh: batch: 16 (over z, y, core), seq: 2 (over x).
Axes of the slice: x: 2, y: 2, z: 4, core: 2. Of those that a mesh axis runs over, the one named last changes fastest.
Arguments:
- tokens: bfloat16 [32, 1024, 800], P('batch', 'seq'), may hold values from -6 to 6
- cotangent: bfloat16 [32, 1024, 800], P('batch', 'seq'), may hold values from -6 to 6
- doc_starts: int32 [32, 8], P('batch'), may hold values from 0 to 1023, as said below
- enc_first: bfloat16 [320000], P(('batch', 'seq')), may hold values from -0.21875 to 0.21875
- enc_conv: bfloat16 [800000], P(('batch', 'seq')), may hold values from -0.125 to 0.125
- enc_last: bfloat16 [320000], P(('batch', 'seq')), may hold values from -0.3125 to 0.3125
- enc_norm_first: float32 [2, 800], replicated, may hold values from -2 to 2, as said below
- enc_norm_inner: float32 [4, 400], replicated, may hold values from -2 to 2, as said below
- dec_first: bfloat16 [320000], P(('batch', 'seq')), may hold values from -0.21875 to 0.21875
- dec_conv: bfloat16 [480000], P(('batch', 'seq')), may hold values from -0.1875 to 0.1875
- dec_last: bfloat16 [320000], P(('batch', 'seq')), may hold values from -0.3125 to 0.3125
- dec_norm_first: float32 [2, 800], replicated, may hold values from -2 to 2, as said below
- dec_norm_inner: float32 [4, 400], replicated, may hold values from -2 to 2, as said below
Outputs:
- out: bfloat16 [32, 1024, 800], P('batch', 'seq')
- grad_tokens: float32 [32, 1024, 800], P('batch', 'seq')
- grad_enc_first: float32 [320000], P(('batch', 'seq'))
- grad_enc_conv: float32 [800000], P(('batch', 'seq'))
- grad_enc_last: float32 [320000], P(('batch', 'seq'))
- grad_enc_norm_first: float32 [2, 800], replicated
- grad_enc_norm_inner: float32 [4, 400], replicated
- grad_dec_first: float32 [320000], P(('batch', 'seq'))
- grad_dec_conv: float32 [480000], P(('batch', 'seq'))
- grad_dec_last: float32 [320000], P(('batch', 'seq'))
- grad_dec_norm_first: float32 [2, 800], replicated
- grad_dec_norm_inner: float32 [4, 400], replicated
The draws below stay inside these ranges and needn't reach their ends.
Inputs may be any that keep to these rules, and one draw needn't show every extreme that they name: `doc_starts`: each row lists the starts of its 8 documents, never falling, the first one 0; equal starts mean an empty document, and the last document ends at the sequence's end. `enc_norm_inner`: rows 0 and 2 are gains, rows 1 and 3 biases. `enc_norm_first`: row 0 is the gain, row 1 the bias. `dec_norm_inner`: rows 0 and 2 are gains, rows 1 and 3 biases. `dec_norm_first`: row 0 is the gain, row 1 the bias.
All inputs are finite; a program needn't handle non-finite values.
Results may differ from the reference program's by a relative error of at most 0.012.
Values may be sent and summed in bfloat16 or wider, within the bound.
A program may use at most 128 MiB of HBM per device.

```python
import math
import jax
import jax.numpy as jnp
from jax import lax

D = 800
H = 400
ENCODER_TAPS = 5
ENCODER_DILATION = 4
DECODER_TAPS = 3
DECODER_DILATION = 16
DOCS = 8
SEQ_MB = 1
SEG = 512
LENGTH = 1024
SEQS = 32


def draw_norm_rows(key, row_count, column_count):
    gain_key, shift_key = jax.random.split(key)
    gains = jnp.exp(jax.random.uniform(gain_key, (row_count, column_count), jnp.float32, math.log(0.5), math.log(2.0)))
    shifts = jnp.clip(0.5 * jax.random.normal(shift_key, (row_count, column_count), jnp.float32), -2.0, 2.0)
    is_gain = (jnp.arange(row_count) % 2 == 0)[:, None]
    return jnp.where(is_gain, gains, shifts)


def draw_enc_norm_first(key, part):
    return draw_norm_rows(jax.random.fold_in(key, 101), 2, D)


def draw_enc_norm_inner(key, part):
    return draw_norm_rows(jax.random.fold_in(key, 202), 4, H)


def draw_dec_norm_first(key, part):
    return draw_norm_rows(jax.random.fold_in(key, 303), 2, D)


def draw_dec_norm_inner(key, part):
    return draw_norm_rows(jax.random.fold_in(key, 404), 4, H)


def draw_doc_starts(key, part):
    base_key = jax.random.fold_in(key, 505)
    first_key, second_key, narrow_key, pick_key = jax.random.split(base_key, 4)
    first_draw = jax.random.randint(first_key, (SEQS, DOCS - 1), 0, LENGTH - 1)
    second_draw = jax.random.randint(second_key, (SEQS, DOCS - 1), 0, LENGTH - 1)
    wide_cuts = 1 + first_draw * second_draw // (LENGTH - 1)
    narrow_cuts = 1 + jax.random.randint(narrow_key, (SEQS, DOCS - 1), 0, SEG // 2)
    group_size = 2 * SEQ_MB
    picked = jax.random.randint(pick_key, (SEQS // group_size,), 0, group_size)
    row_ids = jnp.arange(SEQS, dtype=jnp.int32)
    chosen = row_ids % group_size == jnp.repeat(picked, group_size)
    cuts = jnp.where(chosen[:, None], narrow_cuts, wide_cuts)
    cuts = jnp.sort(cuts, axis=1)
    return jnp.concatenate([jnp.zeros((SEQS, 1), jnp.int32), cuts.astype(jnp.int32)], axis=1)


def level_of(key, extent, cuts, smallest, top_value):
    def one(dim, parts):
        draws = jax.random.uniform(jax.random.fold_in(jax.random.fold_in(key, 6), dim), (parts,), jnp.float32, smallest / len(cuts), top_value / len(cuts))
        return jnp.repeat(jnp.exp(draws), extent[dim] // parts).reshape((-1,) + (1,) * (len(extent) - dim - 1))

    level = one(*cuts[0])
    for cut in cuts[1:]:
        level = level * one(*cut)
    return level


def noise(rng, extent, scale, reach, shards=(), held_as=jnp.bfloat16):
    entries = scale * jax.random.normal(rng, extent, jnp.float32)
    if shards:
        entries = entries * level_of(rng, extent, shards, -0.22, 0.18)
    return jnp.clip(entries, -reach, reach).astype(held_as)


def setup_inputs(seed: int = 0) -> dict:
    key_list = jax.random.split(jax.random.key(seed), 14)
    tokens = noise(key_list[0], (SEQS, LENGTH, D), 1.0, 6.0, ((0, 16), (1, 2)))
    cotangent = noise(key_list[1], (SEQS, LENGTH, D), 1.0, 6.0, ((0, 16), (1, 2)))
    doc_starts = draw_doc_starts(jax.random.fold_in(key_list[13], 71), 0)
    enc_first = noise(key_list[3], (D * H,), D ** -0.5, 0.21875, ((0, 32),))
    enc_conv = noise(key_list[4], (ENCODER_TAPS * H * H,), (ENCODER_TAPS * H) ** -0.5, 0.125, ((0, 32),))
    enc_last = noise(key_list[5], (H * D,), H ** -0.5, 0.3125, ((0, 32),))
    enc_norm_first = draw_enc_norm_first(jax.random.fold_in(key_list[13], 71), 0)
    enc_norm_inner = draw_enc_norm_inner(jax.random.fold_in(key_list[13], 71), 0)
    dec_first = noise(key_list[8], (D * H,), D ** -0.5, 0.21875, ((0, 32),))
    dec_conv = noise(key_list[9], (DECODER_TAPS * H * H,), (DECODER_TAPS * H) ** -0.5, 0.1875, ((0, 32),))
    dec_last = noise(key_list[10], (H * D,), H ** -0.5, 0.3125, ((0, 32),))
    dec_norm_first = draw_dec_norm_first(jax.random.fold_in(key_list[13], 71), 0)
    dec_norm_inner = draw_dec_norm_inner(jax.random.fold_in(key_list[13], 71), 0)
    return dict(tokens=tokens, cotangent=cotangent, doc_starts=doc_starts, enc_first=enc_first, enc_conv=enc_conv, enc_last=enc_last, enc_norm_first=enc_norm_first, enc_norm_inner=enc_norm_inner, dec_first=dec_first, dec_conv=dec_conv, dec_last=dec_last, dec_norm_first=dec_norm_first, dec_norm_inner=dec_norm_inner)


@jax.custom_vjp
def low(v):
    return lax.optimization_barrier(v.astype(jnp.bfloat16)).astype(jnp.float32)

@jax.custom_vjp
def low_back(v):
    return v

def low_keep(v):
    return (low(v), None)

def low_pass(kept, grad):
    return (grad,)

def back_keep(v):
    return (v, None)

def back_low(kept, grad):
    return (low(grad),)
low.defvjp(low_keep, low_pass)
low_back.defvjp(back_keep, back_low)
norm_eps = 1e-05
highest = lax.Precision.HIGHEST

def norm_act(value_rows, norm_gain, norm_shift):
    centre = lax.optimization_barrier(jnp.mean(value_rows, axis=-1, keepdims=True))
    centred = value_rows - centre
    spread = lax.optimization_barrier(jnp.mean(centred * centred, axis=-1, keepdims=True))
    normed = centred * lax.rsqrt(spread + norm_eps)
    return jax.nn.gelu(normed * norm_gain + norm_shift, approximate=False)

def doc_bounds(document_heads, places, length):
    before = document_heads[:, None, :] <= places[None, :, None]
    doc_begin = lax.optimization_barrier(jnp.max(jnp.where(before, document_heads[:, None, :], 0), axis=-1))
    doc_end = lax.optimization_barrier(jnp.min(jnp.where(before, length, document_heads[:, None, :]), axis=-1))
    return (doc_begin, doc_end)

def conv_taps(activated, conv_mat, document_heads, dilation, causal):
    seq_count, length, inner_width = activated.shape
    tap_count = conv_mat.shape[0]
    if causal:
        reach_left = (tap_count - 1) * dilation
        reach_right = 0
    else:
        reach_left = tap_count // 2 * dilation
        reach_right = reach_left
    padded = jnp.pad(activated, ((0, 0), (reach_left, reach_right), (0, 0)))
    places = jnp.arange(length, dtype=jnp.int32)
    doc_begin, doc_end = doc_bounds(document_heads, places, length)
    total = jnp.zeros((seq_count, length, conv_mat.shape[2]), jnp.float32)
    for number_count in range(tap_count):
        if causal:
            offset = (number_count - tap_count + 1) * dilation
        else:
            offset = (number_count - tap_count // 2) * dilation
        window = padded[:, reach_left + offset:reach_left + offset + length]
        source = places[None, :] + offset
        inside = ((source >= doc_begin) & (source < doc_end)).astype(jnp.float32)[:, :, None]
        total = total + inside * jnp.einsum('slh,hk->slk', window, conv_mat[number_count], precision=highest)
    return total

def residual_unit(block_in, first_mat, conv_mat, last_mat, norm_first, norm_inner, document_heads, dilation, causal):
    lowered = low(norm_act(block_in, norm_first[0], norm_first[1]))
    projected = low_back(jnp.einsum('slh,hk->slk', lowered, first_mat, precision=highest))
    activated = low(norm_act(projected, norm_inner[0], norm_inner[1]))
    convolved = low_back(conv_taps(activated, conv_mat, document_heads, dilation, causal))
    mixed = low(norm_act(convolved, norm_inner[2], norm_inner[3]))
    branch = low_back(jnp.einsum('slh,hk->slk', mixed, last_mat, precision=highest))
    return block_in + branch

def reference(tokens, cotangent, doc_starts, enc_first, enc_conv, enc_last, enc_norm_first, enc_norm_inner, dec_first, dec_conv, dec_last, dec_norm_first, dec_norm_inner):
    params = (enc_first.astype(jnp.float32).reshape(D, H), enc_conv.astype(jnp.float32).reshape(ENCODER_TAPS, H, H), enc_last.astype(jnp.float32).reshape(H, D), enc_norm_first.astype(jnp.float32), enc_norm_inner.astype(jnp.float32), dec_first.astype(jnp.float32).reshape(D, H), dec_conv.astype(jnp.float32).reshape(DECODER_TAPS, H, H), dec_last.astype(jnp.float32).reshape(H, D), dec_norm_first.astype(jnp.float32), dec_norm_inner.astype(jnp.float32))

    def group_step(totals, batch_part):
        group_in, group_grad, document_heads = batch_part

        def forward_pass(value_rows, weight_tuple):
            middle_hidden = residual_unit(value_rows, weight_tuple[0], weight_tuple[1], weight_tuple[2], weight_tuple[3], weight_tuple[4], document_heads, ENCODER_DILATION, False)
            return residual_unit(middle_hidden, weight_tuple[5], weight_tuple[6], weight_tuple[7], weight_tuple[8], weight_tuple[9], document_heads, DECODER_DILATION, True)
        result, pullback = jax.vjp(forward_pass, group_in.astype(jnp.float32), params)
        grad_in, grad_weights = pullback(group_grad.astype(jnp.float32))
        totals = jax.tree.map(lambda former, latter: former + latter, totals, grad_weights)
        return (totals, (result.astype(jnp.bfloat16), grad_in))
    zero_totals = jax.tree.map(jnp.zeros_like, params)
    inputs = (tokens.reshape(SEQS, 1, LENGTH, D), cotangent.reshape(SEQS, 1, LENGTH, D), doc_starts.reshape(SEQS, 1, DOCS))
    totals, (outputs, grad_inputs) = lax.scan(group_step, zero_totals, inputs)
    return (outputs.reshape(SEQS, LENGTH, D), grad_inputs.reshape(SEQS, LENGTH, D), totals[0].reshape(-1), totals[1].reshape(-1), totals[2].reshape(-1), totals[3], totals[4], totals[5].reshape(-1), totals[6].reshape(-1), totals[7].reshape(-1), totals[8], totals[9])
```

```python
import functools
import types

import jax
import jax.numpy as jnp
from jax import lax
from jax.experimental import pallas as pl
from jax.experimental.pallas import tpu as pltpu
from jax.sharding import PartitionSpec as P

H = 400
ENCODER_TAPS = 5
ENCODER_DILATION = 4
DECODER_TAPS = 3
DECODER_DILATION = 16

F32, BF16 = jnp.float32, jnp.bfloat16
MESH = pl.DeviceIdType.MESH
LANES = 128
TILES = 4
CHUNK = 16
REACH = 32
SHARE = 112
SLACK = 8
EPS = 1e-5
HI, LO, CORE, SEQ = 0, 1, 2, 3
ORDER_A = (HI, LO, SEQ, CORE)
ORDER_C = (SEQ, HI, LO, CORE)
LAG = 2


def round_up(value, step):
    return -(-value // step) * step


class Grid:
    def __init__(self, mesh):
        batch, seq = mesh.shape["batch"], mesh.shape["seq"]
        lo = 2 if batch <= 16 else 4
        self.sizes = (batch // (2 * lo), lo, 2, seq)
        self.count = batch * seq

    def own(self):
        batch = lax.axis_index("batch")
        lo = self.sizes[1]
        return (batch // (2 * lo), (batch // 2) % lo, batch % 2, lax.axis_index("seq"))

    def device(self, place):
        hi, lo, core, seq = place
        return ((hi * self.sizes[1] + lo) * 2 + core, seq)

    def peer(self, own, dim, distance):
        place = list(own)
        place[dim] = lax.rem(own[dim] + distance, self.sizes[dim])
        return tuple(place)

    def slot(self, dim, distance):
        return sum(size - 1 for size in self.sizes[:dim]) + distance - 1

    def slots(self):
        return sum(size - 1 for size in self.sizes)


def split_rows(rows):
    first = round_up(int(rows * 0.6), 16)
    parts = [(0, first, ORDER_A)]
    if first < rows:
        parts.append((first, rows - first, ORDER_C))
    return parts


def remote(source, target, send, receive, device):
    copy = pltpu.make_async_remote_copy(
        source, target, send, receive, device_id=device, device_id_type=MESH
    )
    copy.start()
    return copy


class Gather:
    def __init__(self, grid, own, held, send, receive, rows):
        self.grid, self.own, self.held = grid, own, held
        self.send, self.receive = send, receive
        self.parts = split_rows(rows)
        self.copies = {}

    def start(self, stage):
        for color, (begin, count, order) in enumerate(self.parts):
            dim, done = order[stage], order[:stage]
            index = tuple(slice(None) if d in done else self.own[d] for d in range(4))
            block = self.held.at[index + (pl.ds(begin, count),)]
            copies = []
            for distance in range(1, self.grid.sizes[dim]):
                slot = self.grid.slot(dim, distance)
                target = self.grid.device(self.grid.peer(self.own, dim, distance))
                copies.append(
                    remote(
                        block,
                        block,
                        self.send.at[color, slot],
                        self.receive.at[color, slot],
                        target,
                    )
                )
            self.copies[color, stage] = copies

    def arrive(self, stage):
        for color in range(len(self.parts)):
            for copy in self.copies[color, stage]:
                copy.wait_recv()

    def leave(self):
        for copies in self.copies.values():
            for copy in copies:
                copy.wait_send()


def landing_shapes(grid, rows):
    shapes = []
    for begin, count, order in split_rows(rows):
        back = order[::-1]
        for stage, dim in enumerate(back):
            rest = tuple(grid.sizes[d] for d in range(4) if d not in back[: stage + 1])
            shapes.append((grid.sizes[dim] - 1,) + rest + (count, LANES))
    return shapes


class Scatter:
    def __init__(self, grid, own, held, landing, send, receive, rows, result):
        self.grid, self.own, self.held, self.landing = grid, own, held, landing
        self.send, self.receive, self.result = send, receive, result
        self.parts = split_rows(rows)
        self.copies = {}
        self.stage = 0

    def start(self):
        for color, (begin, count, order) in enumerate(self.parts):
            back = order[::-1]
            dim, done = back[self.stage], back[: self.stage]
            copies = []
            for distance in range(1, self.grid.sizes[dim]):
                place = self.grid.peer(self.own, dim, distance)
                index = tuple(
                    self.own[d] if d in done else place[d] if d == dim else slice(None)
                    for d in range(4)
                )
                slot = self.grid.slot(dim, distance)
                copies.append(
                    remote(
                        self.held.at[index + (pl.ds(begin, count),)],
                        self.landing[color * 4 + self.stage].at[distance - 1],
                        self.send.at[color, slot],
                        self.receive.at[color, slot],
                        self.grid.device(place),
                    )
                )
            self.copies[color, self.stage] = copies

    def finish(self):
        for color, (begin, count, order) in enumerate(self.parts):
            back = order[::-1]
            done = back[: self.stage + 1]
            rest = [d for d in range(4) if d not in done]
            for copy in self.copies[color, self.stage]:
                copy.wait_recv()
            landing = self.landing[color * 4 + self.stage]
            senders = landing.shape[0]
            blocks = 1
            for d in rest:
                blocks *= self.grid.sizes[d]

            def add(block, carry, begin=begin, count=count, landing=landing, rest=rest):
                left, place = block, {}
                for d in reversed(rest):
                    place[d] = left % self.grid.sizes[d]
                    left = left // self.grid.sizes[d]
                index = tuple(place.get(d, self.own[d]) for d in range(4))
                total = self.held[index + (pl.ds(begin, count),)].astype(F32)
                for sender in range(senders):
                    where = (sender,) + tuple(place[d] for d in rest)
                    total = total + landing[where].astype(F32)
                if rest:
                    self.held[index + (pl.ds(begin, count),)] = total.astype(BF16)
                else:
                    self.result[pl.ds(begin, count), :] = total
                return carry

            if blocks == 1:
                add(0, 0)
            else:
                lax.fori_loop(0, blocks, add, 0, unroll=2 if blocks % 2 == 0 else 1)
        self.stage += 1

    def leave(self):
        for copies in self.copies.values():
            for copy in copies:
                copy.wait_send()


class Reduce:
    ORDER = (CORE, SEQ, LO, HI)

    def __init__(self, grid, own, slots, send, receive):
        self.grid, self.own, self.slots = grid, own, slots
        self.send, self.receive = send, receive
        self.copies = {}
        self.stage = 0

    def start(self, value=None):
        dim = self.ORDER[self.stage]
        slots, mine = self.slots[dim], self.own[dim]
        if value is not None:
            slots[mine] = value
        self.copies[self.stage] = [
            remote(
                slots.at[mine],
                slots.at[mine],
                self.send.at[self.grid.slot(dim, distance)],
                self.receive.at[self.grid.slot(dim, distance)],
                self.grid.device(self.grid.peer(self.own, dim, distance)),
            )
            for distance in range(1, self.grid.sizes[dim])
        ]

    def finish(self):
        dim = self.ORDER[self.stage]
        for copy in self.copies[self.stage]:
            copy.wait_recv()
        total = self.slots[dim][0]
        for other in range(1, self.grid.sizes[dim]):
            total = total + self.slots[dim][other]
        self.stage += 1
        if self.stage < 4:
            following = self.ORDER[self.stage]
            self.slots[following][self.own[following]] = total
        else:
            self.result = total

    def leave(self):
        for copies in self.copies.values():
            for copy in copies:
                copy.wait_send()


def lane_ids(rows):
    return lax.broadcasted_iota(jnp.int32, (rows, LANES), 1)


def period_of(elements):
    group = 1
    while (group * elements) % H:
        group *= 2
    return group


class Pieces:
    def __init__(self, grid, elements):
        self.grid, self.elements = grid, elements
        self.rows = round_up(-(-elements // LANES), 16)
        self.pitch = self.rows + SLACK
        self.group = period_of(elements)
        self.groups = grid.count // self.group
        self.period = self.group * elements // H
        self.passes = 2 if self.groups % 16 == 0 else 1
        self.matrix_rows = grid.count * elements // H
        self.part_rows = self.matrix_rows // self.passes

    def flat_rows(self):
        return self.grid.count // self.passes * self.pitch + SLACK

    def each(self, held, flat, part, widen):
        _, lo, core, seq = self.grid.sizes
        count = self.grid.count // self.passes

        def body(local, carry):
            piece = local + part * count
            index = (piece // (lo * core * seq), (piece // (core * seq)) % lo, (piece // seq) % core, piece % seq)
            begin = pl.multiple_of(local * self.pitch + SLACK, SLACK)
            if widen:
                flat[pl.ds(begin, self.rows), :] = held[index].astype(F32)
            else:
                held[index] = flat[pl.ds(begin, self.rows), :].astype(BF16)
            return carry

        lax.fori_loop(0, count, body, 0, unroll=4)

    def at(self, piece, row):
        count = self.groups // self.passes
        return (pl.ds(piece * self.pitch + row, count, stride=self.group * self.pitch), slice(None))

    def row_at(self, row, lead=0):
        count = self.groups // self.passes
        return (pl.ds(row + lead, count, stride=self.period), slice(None))

    def unpack(self, held, flat, matrix, part, lead):
        lane = lane_ids(self.groups // self.passes)
        self.each(held, flat, part, True)
        for piece in range(self.group):
            offset = piece * self.elements
            first, last = -(-offset // H), (offset + self.elements) // H

            def body(row, carry, piece=piece, offset=offset):
                local = row * H - offset + SLACK * LANES
                source, shift = local // LANES, local % LANES
                keep = lane < LANES - shift
                back = lax.rem(LANES - shift, LANES)
                rolled = [
                    pltpu.roll(flat[self.at(piece, source + t)], back, axis=1)
                    for t in range(TILES + 1)
                ]
                for tile in range(TILES):
                    matrix.at[tile][self.row_at(row, lead)] = jnp.where(
                        keep, rolled[tile], rolled[tile + 1]
                    )
                return carry

            if last > first:
                lax.fori_loop(first, last, body, 0, unroll=last - first)
            if (offset + self.elements) % H:
                self.shared_row(flat, matrix, piece, last, lane, lead)

    def shared_row(self, flat, matrix, piece, row, lane, lead):
        local = row * H - piece * self.elements
        cut = (piece + 1) * self.elements - row * H
        for tile in range(TILES):
            begin, end = tile * LANES, min((tile + 1) * LANES, H)
            value = jnp.zeros(lane.shape, F32)
            position = begin
            while position < end:
                if position < cut:
                    owner, at, stop = piece, local + position, min(end, cut)
                else:
                    owner, at, stop = piece + 1, position - cut, end
                source, slot = at // LANES + SLACK, at % LANES
                stop = min(stop, position + LANES - slot)
                goal = position - begin
                rolled = pltpu.roll(flat[self.at(owner, source)], (goal - slot) % LANES, axis=1)
                value = jnp.where((lane >= goal) & (lane < goal + stop - position), rolled, value)
                position = stop
            matrix.at[tile][self.row_at(row, lead)] = value

    def pack(self, matrix, flat, held, part):
        lane = lane_ids(self.groups // self.passes)
        for piece in range(self.group):
            offset = piece * self.elements
            first, last = offset // H, -(-(offset + self.elements) // H)

            def body(row, pending, piece=piece, offset=offset):
                local = row * H - offset + SLACK * LANES
                target, shift = local // LANES, local % LANES
                keep = lane >= shift
                rolled = [
                    pltpu.roll(matrix.at[tile][self.row_at(row)], shift, axis=1) for tile in range(TILES)
                ]
                before = pending
                for tile in range(TILES):
                    value = jnp.where(keep, rolled[tile], before)
                    flat[self.at(piece, target + tile)] = value
                    before = rolled[tile]
                return jnp.where(shift + H % LANES > LANES, rolled[-1], value)

            pending = lax.fori_loop(first, last, body, jnp.zeros(lane.shape, F32), unroll=last - first)
            ending = (last * H - offset + SLACK * LANES) // LANES
            flat[self.at(piece, ending)] = pending
        self.each(held, flat, part, False)


def dot(a, b, left, right, precision=None):
    return lax.dot_general(
        a, b, (((left,), (right,)), ((), ())), precision=precision, preferred_element_type=F32
    )


def nn(a, b):
    return dot(a, b, 1, 0)


def nt(a, b):
    return dot(a, b, 1, 1)


def tn(a, b):
    return dot(a, b, 0, 0)


def tile_span(tile, width):
    return tile * LANES, min(LANES, width - tile * LANES)


def chunks(count, body, carry=0, unroll=5):
    def step(index, carry):
        return body(pl.multiple_of(index * CHUNK, CHUNK), carry)

    return lax.fori_loop(0, count // CHUNK, step, carry, unroll=unroll)


def zeros(tiles):
    return (jnp.zeros((CHUNK, LANES), F32),) * tiles


def column_sums(totals, count):
    return [jnp.sum(total, axis=0, keepdims=True) * (1.0 / count) for total in totals]


def gelu_parts(a):
    bell = jnp.exp(a * a * -0.5)
    t = 1.0 / (1.0 + jnp.abs(a) * (0.3275911 * 0.7071067811865476))
    poly = 1.061405429 * t - 1.453152027
    poly = ((poly * t + 1.421413741) * t - 0.284496736) * t + 0.254829592
    tail = poly * t * bell * 0.5
    phi = jnp.where(a >= 0.0, 1.0 - tail, tail)
    return a * phi, phi + a * bell * 0.3989422804014327


class Block:
    def __init__(self, index, offsets, norms):
        self.index, self.offsets = index, offsets
        self.before, self.after = min(offsets) < 0, max(offsets) > 0
        self.norms = norms


ENCODER = Block(
    0, [(j - ENCODER_TAPS // 2) * ENCODER_DILATION for j in range(ENCODER_TAPS)], (0, 1)
)
DECODER = Block(1, [(j - DECODER_TAPS + 1) * DECODER_DILATION for j in range(DECODER_TAPS)], (2, 3))
BLOCKS = (ENCODER, DECODER)
FIRST, CONV, LAST = 0, 1, 2
OUTER, P_NORM, C_NORM = 0, 1, 2


def spaces(tree):
    if isinstance(tree, dict):
        return types.SimpleNamespace(**{key: spaces(value) for key, value in tree.items()})
    if isinstance(tree, (list, tuple)):
        return [spaces(value) for value in tree]
    return tree


class Plan:
    def __init__(self, grid, seqs, seg, width, elements):
        self.grid, self.seqs, self.seg, self.width = grid, seqs, seg, width
        self.rows = seqs * seg
        self.tiles = seg // LANES
        self.pieces = [Pieces(grid, count) for count in elements]
        self.norm_tiles = -(-width // LANES)
        sizes = [p.rows for p in self.pieces] + [8 * self.norm_tiles] * 2
        self.small_at = [sum(sizes[:k]) for k in range(len(sizes) + 1)]
        vmem, dma = pltpu.VMEM, pltpu.SemaphoreType.DMA
        rows, count = self.rows, len(elements)

        def block(which):
            taps = len(which.offsets)
            half = dict(
                normed=vmem((H, rows), BF16), slope=vmem((H, rows), BF16), value=vmem((H, rows), BF16)
            )
            return dict(
                weights=[vmem((width, H), BF16), vmem((taps * H, H), BF16), vmem((H, width), BF16)],
                acts=[dict(slope=vmem((width, rows), BF16), value=vmem((width, rows), BF16)), half, half],
                halo=[[vmem((2, seqs, SHARE, LANES), BF16) for _ in range(2)] for _ in range(2)],
                stats=vmem((8, rows), F32),
                outer=vmem((2, width, LANES), F32),
                inner=vmem((4, H, LANES), F32),
                sums=vmem((8, width), F32),
                slots=[vmem((size, 8, width), F32) for size in grid.sizes],
            )

        self.scratch = dict(
            held=[vmem(grid.sizes + (p.rows, LANES), BF16) for p in self.pieces],
            landing=[[vmem(shape, BF16) for shape in landing_shapes(grid, p.rows)] for p in self.pieces],
            flat=vmem((max(p.flat_rows() for p in self.pieces), LANES), F32),
            matrix=vmem((TILES, max(p.part_rows for p in self.pieces) + 16, LANES), F32),
            blocks=[block(which) for which in BLOCKS],
            given=vmem((width, rows), BF16),
            total=vmem((width, rows), F32),
            staged=vmem((width, seg), BF16),
            wide=vmem((seqs, H, seg + 2 * LANES), BF16),
            begin=vmem((seqs, CHUNK, seg + 2 * LANES), jnp.int32),
            taps=vmem((ENCODER_TAPS * H, rows), BF16),
            broad=vmem((width, seg), F32),
            spread=vmem((2, width, LANES), F32),
            last_grad=vmem((-(-width // LANES), H, LANES), F32),
            local_sem=dma((count + 2 * seqs + 2,)),
            gather_sem=dma((2, count, 2, grid.slots())),
            scatter_sem=dma((2, count, 2, grid.slots())),
            reduce_sem=dma((2, 2, grid.slots())),
            halo_sem=dma((2, 4, seqs, 2)),
        )


class Kernel:
    def __init__(self, plan, ins, outs, scratch):
        self.plan, self.grid, self.own = plan, plan.grid, plan.grid.own()
        self.ins, self.outs, self.s = ins, outs, scratch
        self.in_flight, self.scatters, self.reduces = [], [], []


    def signal_entry(self):
        barrier = pltpu.get_barrier_semaphore()
        for dim in range(4):
            for distance in range(1, self.grid.sizes[dim]):
                pl.semaphore_signal(
                    barrier,
                    inc=1,
                    device_id=self.grid.device(self.grid.peer(self.own, dim, distance)),
                    device_id_type=MESH,
                )

    def wait_entry(self):
        pl.semaphore_wait(pltpu.get_barrier_semaphore(), self.grid.slots())

    def open_gathers(self):
        self.gathers = [
            Gather(
                self.grid,
                self.own,
                self.s.held[k],
                self.s.gather_sem.at[0, k],
                self.s.gather_sem.at[1, k],
                pieces.rows,
            )
            for k, pieces in enumerate(self.plan.pieces)
        ]
        self.step = 0

    def gather_step(self):
        t, count = self.step, len(self.gathers)
        if t >= count + 4 * LAG:
            return
        for stage in reversed(range(4)):
            k = t - LAG * (stage + 1)
            if 0 <= k < count:
                self.gathers[k].arrive(stage)
                if stage < 3:
                    self.gathers[k].start(stage + 1)
        if t < count:
            self.gathers[t].start(0)
        self.step += 1

    def gather_until(self, k):
        while self.step <= k + 4 * LAG:
            self.gather_step()

    def tick(self):
        for item in list(self.in_flight):
            item.finish()
            if item.stage < 4:
                item.start()
            else:
                self.in_flight.remove(item)

    def scatter(self, k):
        item = Scatter(
            self.grid,
            self.own,
            self.s.held[k],
            self.s.landing[k],
            self.s.scatter_sem.at[0, k],
            self.s.scatter_sem.at[1, k],
            self.plan.pieces[k].rows,
            self.outs.small.at[pl.ds(self.plan.small_at[k], self.plan.pieces[k].rows)],
        )
        item.start()
        self.in_flight.append(item)
        self.scatters.append(item)

    def reduce(self, block):
        k, refs = block.index, self.s.blocks[block.index]
        item = Reduce(
            self.grid, self.own, refs.slots, self.s.reduce_sem.at[0, k], self.s.reduce_sem.at[1, k]
        )
        item.start(refs.sums[...])
        self.in_flight.append(item)
        self.reduces.append(item)

    def send_halo(self, block, way, s):
        seg, size, way_refs = self.plan.seg, self.grid.sizes[SEQ], self.s.blocks[block.index].halo[way]
        before, after = (block.after, block.before) if way else (block.before, block.after)
        copies = []
        for side, wanted, begin, distance in ((0, before, seg, 1), (1, after, LANES, size - 1)):
            if wanted:
                phase = 2 * block.index + way
                message = way_refs[side].at[0, s]
                self.pack_halo(s, begin, LANES - REACH if side == 0 else 0, message)
                copy = remote(
                    message,
                    way_refs[side].at[1, s],
                    self.s.halo_sem.at[0, phase, s, side],
                    self.s.halo_sem.at[1, phase, s, side],
                    self.grid.device(self.grid.peer(self.own, SEQ, distance)),
                )
                copies.append((side, copy))
        return copies

    def shares(self):
        return [(quarter, begin, min(SHARE, H - begin)) for quarter, begin in enumerate(range(0, H, SHARE))]

    def pack_halo(self, s, begin, lane, message):
        lanes = lane_ids(SHARE)
        total = jnp.zeros((SHARE, LANES), F32)
        for quarter, row, rows in self.shares():
            value = self.s.wide[s, row : row + rows, begin : begin + LANES].astype(F32)
            if rows < SHARE:
                value = jnp.concatenate([value, jnp.zeros((SHARE - rows, LANES), F32)], axis=0)
            value = pltpu.roll(value, (quarter * REACH - lane) % LANES, axis=1)
            total = jnp.where(lanes >= quarter * REACH, value, total)
        message[...] = total.astype(BF16)

    def take_halo(self, block, way, s, copies):
        for side, copy in copies:
            copy.wait()
            begin = (self.plan.seg + LANES) if side else 0
            lane = 0 if side else LANES - REACH
            message = self.s.blocks[block.index].halo[way][side][1, s].astype(F32)
            for quarter, row, rows in self.shares():
                value = pltpu.roll(message, (lane - quarter * REACH) % LANES, axis=1)
                self.s.wide[s, row : row + rows, begin : begin + LANES] = value[0:rows].astype(BF16)


    def unpack(self, k):
        self.gather_until(k)
        pieces, matrix, step = self.plan.pieces[k], self.s.matrix, 32 if k % 3 == LAST else 16
        lead = 0
        for part in range(pieces.passes):
            pieces.unpack(self.s.held[k], self.s.flat, matrix, part, lead)
            ready = (lead + pieces.part_rows) // step * step
            self.convert(k, part * pieces.part_rows - lead, ready)
            lead = lead + pieces.part_rows - ready
            if lead:
                matrix[:, 0:lead, :] = matrix[:, ready : ready + lead, :]

    def convert(self, k, base, rows):
        target = self.s.blocks[k // 3].weights[k % 3]
        matrix, chunk = self.s.matrix, 16
        if k % 3 == LAST:
            keep = lane_ids(chunk) < H % LANES

            def body(index, carry):
                r = pl.multiple_of(index * chunk, 16)
                left = [matrix.at[c][pl.ds(2 * r, chunk, stride=2), :] for c in range(TILES)]
                right = [
                    pltpu.roll(matrix.at[c][pl.ds(2 * r + 1, chunk, stride=2), :], H % LANES, axis=1)
                    for c in range(TILES)
                ]
                tiles = left[:3] + [jnp.where(keep, left[3], right[0])]
                tiles += [jnp.where(keep, right[c], right[c + 1]) for c in range(3)]
                for c, value in enumerate(tiles):
                    begin, size = tile_span(c, target.shape[1])
                    goal = pl.multiple_of(base // 2 + r, 16)
                    target[pl.ds(goal, chunk), begin : begin + size] = value[:, :size].astype(BF16)
                return carry

            lax.fori_loop(0, rows // (2 * chunk), body, 0, unroll=4)
        else:

            def body(index, carry):
                r = pl.multiple_of(index * chunk, 16)
                goal = pl.multiple_of(base + r, 16)
                for c in range(TILES):
                    begin, size = tile_span(c, H)
                    target[pl.ds(goal, chunk), begin : begin + size] = matrix[c, pl.ds(r, chunk), :size].astype(BF16)
                return carry

            lax.fori_loop(0, rows // chunk, body, 0, unroll=4)

    def give(self, k, part):
        pieces = self.plan.pieces[k]
        pieces.pack(self.s.matrix, self.s.flat, self.s.held[k], part)
        if part == pieces.passes - 1:
            self.scatter(k)

    def grad_rows(self, begin, value):
        for c in range(TILES):
            low, size = tile_span(c, H)
            self.s.matrix[c, begin : begin + value.shape[0], 0:size] = value[:, low : low + size]

    def give_rows(self, k, values):
        pieces, broad = self.plan.pieces[k], self.s.broad
        part, room = 0, pieces.part_rows
        for value in values:
            begin = 0
            while begin < H:
                count = min(room, H - begin)
                if begin:
                    self.grad_rows(pieces.part_rows - room, broad[0:count, 0:H])
                else:
                    self.grad_rows(pieces.part_rows - room, value[0:count])
                    if count < H:
                        broad[0 : H - count, 0:H] = value[count:]
                begin, room = begin + count, room - count
                if not room:
                    self.give(k, part)
                    part, room = part + 1, pieces.part_rows

    def give_last(self, k, value):
        width, matrix, chunk = self.plan.width, self.s.matrix, 40
        pieces, store = self.plan.pieces[k], self.s.last_grad
        tiles_of = -(-width // LANES)
        for c in range(tiles_of):
            begin, size = tile_span(c, width)
            store[c, :, 0:size] = value[:, begin : begin + size]
        keep = lane_ids(chunk) < LANES - H % LANES
        for part in range(pieces.passes):
            base = part * pieces.part_rows // 2

            def body(index, carry, base=base):
                r = pl.multiple_of(index * chunk, 8)
                rows = pl.ds(pl.multiple_of(base + r, 8), chunk)
                tiles = [store[c, rows, :] for c in range(tiles_of)]
                for c in range(TILES):
                    matrix.at[c][pl.ds(2 * r, chunk, stride=2), :] = tiles[c]
                back = [pltpu.roll(value, LANES - H % LANES, axis=1) for value in tiles[3:]]
                back.append(back[-1])
                for c in range(TILES):
                    matrix.at[c][pl.ds(2 * r + 1, chunk, stride=2), :] = jnp.where(keep, back[c], back[c + 1])
                return carry

            lax.fori_loop(0, pieces.part_rows // (2 * chunk), body, 0)
            self.give(k, part)


    def documents(self):
        seg, span = self.plan.seg, self.plan.seg + 2 * LANES
        whole = seg * self.grid.sizes[SEQ]
        place = lax.broadcasted_iota(jnp.int32, (CHUNK, span), 1) + (self.own[SEQ] * seg - LANES)
        for s in range(self.plan.seqs):
            begin = jnp.zeros((CHUNK, span), jnp.int32)
            for k in range(self.ins.doc_starts.shape[1]):
                head = self.ins.doc_starts[s, k]
                begin = jnp.maximum(begin, jnp.where(place >= head, head, 0))
            begin = jnp.where(place < 0, -1, begin)
            self.s.begin[s] = jnp.where(place >= whole, -2, begin)

    def shifted(self, tiles, shift, lane):
        count = len(tiles) - 2
        if not shift:
            return tiles[1:-1]
        rolled = [pltpu.roll(tile, -shift % LANES, axis=1) for tile in tiles]
        if shift > 0:
            return [jnp.where(lane < LANES - shift, rolled[c + 1], rolled[c + 2]) for c in range(count)]
        return [jnp.where(lane >= -shift, rolled[c + 1], rolled[c]) for c in range(count)]

    def spread_taps(self, block, s, sign):
        count, seg, wide, taps = self.plan.tiles, self.plan.seg, self.s.wide, self.s.taps
        lane = lane_ids(CHUNK)
        heads = [self.s.begin[s, :, t * LANES : (t + 1) * LANES] for t in range(count + 2)]
        inside = [
            [there == here for there, here in zip(self.shifted(heads, sign * offset, lane), heads[1:-1])]
            for offset in block.offsets
        ]

        def body(r, carry):
            tiles = [wide[s, pl.ds(r, CHUNK), t * LANES : (t + 1) * LANES].astype(F32) for t in range(count + 2)]
            for j, offset in enumerate(block.offsets):
                for t, value in enumerate(self.shifted(tiles, sign * offset, lane)):
                    if offset:
                        value = jnp.where(inside[j][t], value, 0.0)
                    begin = s * seg + t * LANES
                    taps[pl.ds(pl.multiple_of(j * H + r, CHUNK), CHUNK), begin : begin + LANES] = value.astype(BF16)
            return carry

        chunks(H, body)


    def norm_columns(self):
        for block in BLOCKS:
            refs = self.s.blocks[block.index]
            for source, target in zip(block.norms, (refs.outer, refs.inner)):
                rows = self.ins.norms[source]
                for k in range(rows.shape[0]):
                    for tile in range(-(-rows.shape[1] // LANES)):
                        begin, size = tile_span(tile, rows.shape[1])
                        row = rows[k : k + 1, begin : begin + size]
                        target[k, begin : begin + size, :] = jnp.broadcast_to(row, (LANES, size)).T

    def gains(self, block, norm):
        refs = self.s.blocks[block.index]
        if norm == OUTER:
            return refs.outer.at[0], refs.outer.at[1]
        return refs.inner.at[2 * norm - 2], refs.inner.at[2 * norm - 1]

    def lanes_of(self, s, t=None):
        if t is None:
            return slice(s * self.plan.seg, (s + 1) * self.plan.seg)
        begin = s * self.plan.seg + t * LANES
        return slice(begin, begin + LANES)

    def act(self, block, norm, s, count, load, wide=False):
        tiles = range(self.plan.tiles)
        refs = self.s.blocks[block.index]
        act, stats = refs.acts[norm], refs.stats
        gain, shift = self.gains(block, norm)

        def first(r, carry):
            rows = pl.ds(r, CHUNK)
            return tuple(carry[t] + load(rows, t, True) for t in tiles)

        centre = column_sums(chunks(count, first, zeros(len(tiles))), count)

        def second(r, carry):
            rows, out = pl.ds(r, CHUNK), []
            for t in tiles:
                away = load(rows, t) - centre[t]
                out.append(carry[t] + away * away)
            return tuple(out)

        spread = column_sums(chunks(count, second, zeros(len(tiles))), count)
        scale = [lax.rsqrt(value + EPS) for value in spread]

        def third(r, carry):
            rows = pl.ds(r, CHUNK)
            g, b = gain[rows, :], shift[rows, :]
            for t in tiles:
                lanes = self.lanes_of(s, t)
                normed = (load(rows, t) - centre[t]) * scale[t]
                value, slope = gelu_parts(normed * g + b)
                value = value.astype(BF16)
                act.value[rows, lanes] = value
                act.slope[rows, lanes] = slope.astype(BF16)
                if norm != OUTER:
                    act.normed[rows, lanes] = normed.astype(BF16)
                if wide:
                    self.s.wide[s, rows, (t + 1) * LANES : (t + 2) * LANES] = value
            return carry

        chunks(count, third)
        for t in tiles:
            lanes = self.lanes_of(s, t)
            if norm == OUTER:
                stats[0:1, lanes] = centre[t]
            stats[norm + 1 : norm + 2, lanes] = scale[t]

    def act_back(self, block, norm, s, count, store):
        tiles = range(self.plan.tiles)
        refs, broad, spread = self.s.blocks[block.index], self.s.broad, self.s.spread
        act, stats = refs.acts[norm], refs.stats
        gain, _ = self.gains(block, norm)
        scale = [stats[norm + 1 : norm + 2, self.lanes_of(s, t)] for t in tiles]
        centre = [stats[0:1, self.lanes_of(s, t)] for t in tiles]

        def normed(rows, t):
            if norm == OUTER:
                return (self.x_in(block, rows, self.lanes_of(s, t)) - centre[t]) * scale[t]
            return act.normed[rows, self.lanes_of(s, t)].astype(F32)

        def first(r, carry):
            rows = pl.ds(r, CHUNK)
            g = gain[rows, :]
            ones, twos = [], []
            for t in tiles:
                e = broad[rows, t * LANES : (t + 1) * LANES] * act.slope[rows, self.lanes_of(s, t)].astype(F32)
                n = normed(rows, t)
                en, weighted = e * n, e * g
                ones.append(carry[0][t] + weighted)
                twos.append(carry[1][t] + weighted * n)
                gains, shifts = (gains + en, shifts + e) if t else (en, e)
            if s:
                gains, shifts = gains + spread[0, rows, :], shifts + spread[1, rows, :]
            spread[0, rows, :] = gains
            spread[1, rows, :] = shifts
            return tuple(ones), tuple(twos)

        ones, twos = chunks(count, first, (zeros(len(tiles)), zeros(len(tiles))))
        ones, twos = column_sums(ones, count), column_sums(twos, count)

        def second(r, carry):
            rows = pl.ds(r, CHUNK)
            g = gain[rows, :]
            for t in tiles:
                lanes = self.lanes_of(s, t)
                weighted = broad[rows, t * LANES : (t + 1) * LANES] * act.slope[rows, lanes].astype(F32) * g
                store(rows, t, (weighted - ones[t] - normed(rows, t) * twos[t]) * scale[t])
            return carry

        chunks(count, second)

    def norm_grads(self, block, norm, count):
        sums = self.s.blocks[block.index].sums
        for k in range(2):
            for tile in range(-(-count // LANES)):
                begin, size = tile_span(tile, count)
                block_rows = self.s.spread[k, begin : begin + size, :].T
                sums[2 * norm + k : 2 * norm + k + 1, begin : begin + size] = jnp.sum(
                    block_rows, axis=0, keepdims=True
                )


    def from_broad(self, rows, t, again=False):
        return self.s.broad[rows, t * LANES : (t + 1) * LANES]

    def forward_inner(self, block):
        refs, broad = self.s.blocks[block.index], self.s.broad
        base, taps = 3 * block.index, len(block.offsets)
        seqs = range(self.plan.seqs)
        self.unpack(base + FIRST)
        halos = []
        for s in seqs:
            broad[0:H, :] = tn(refs.weights[FIRST][...], refs.acts[OUTER].value[:, self.lanes_of(s)])
            self.gather_step()
            self.act(block, P_NORM, s, H, self.from_broad, wide=True)
            halos.append(self.send_halo(block, 0, s))
            self.gather_step()
        self.unpack(base + CONV)
        for s in seqs:
            self.take_halo(block, 0, s, halos[s])
            self.spread_taps(block, s, 1)
            broad[0:H, :] = tn(refs.weights[CONV][...], self.s.taps[0 : taps * H, self.lanes_of(s)])
            self.gather_step()
            self.act(block, C_NORM, s, H, self.from_broad)
            self.gather_step()
        self.unpack(base + LAST)

    def forward(self):
        broad, total, plan = self.s.broad, self.s.total, self.plan
        self.forward_inner(ENCODER)
        for s in range(plan.seqs):
            refs = self.s.blocks[0]
            broad[...] = tn(refs.weights[LAST][...], refs.acts[C_NORM].value[:, self.lanes_of(s)])

            def load(rows, t, fresh=False, s=s):
                lanes = self.lanes_of(s, t)
                if fresh:
                    total[rows, lanes] = self.s.given[rows, lanes].astype(F32) + self.from_broad(rows, t)
                return total[rows, lanes]

            self.act(DECODER, OUTER, s, plan.width, load)
            self.gather_step()
        self.load(self.ins.cotangent)
        self.forward_inner(DECODER)
        for s in range(plan.seqs):
            refs = self.s.blocks[1]
            broad[...] = tn(refs.weights[LAST][...], refs.acts[C_NORM].value[:, self.lanes_of(s)])
            if s:
                copy.wait()

            def finish(r, carry, s=s):
                rows = pl.ds(r, CHUNK)
                value = total[rows, self.lanes_of(s)] + broad[rows, :]
                self.s.staged[rows, :] = value.astype(BF16)
                return carry

            chunks(plan.width, finish)
            copy = pltpu.make_async_copy(self.s.staged, self.outs.out.at[s], self.s.local_sem.at[6])
            copy.start()
        self.storing = copy


    def backward(self, block, dq, finish, ready=None):
        refs, broad, taps = self.s.blocks[block.index], self.s.broad, self.s.taps
        base, seqs = 3 * block.index, range(self.plan.seqs)
        v, w, u = (refs.acts[k].value for k in (P_NORM, C_NORM, OUTER))
        halos = []
        for s in seqs:
            broad[0:H, :] = nn(refs.weights[LAST][...], dq[:, self.lanes_of(s)])

            def store(rows, t, value, s=s):
                self.s.wide[s, rows, (t + 1) * LANES : (t + 2) * LANES] = value.astype(BF16)

            self.act_back(block, C_NORM, s, H, store)
            halos.append(self.send_halo(block, 1, s))
        self.norm_grads(block, C_NORM, H)
        self.tick()
        self.give_last(base + LAST, nt(w[...], dq[...]))
        for s in seqs:
            self.take_halo(block, 1, s, halos[s])
            self.spread_taps(block, s, -1)
        self.tick()
        self.give_rows(
            base + CONV, (nt(v[...], taps[j * H : (j + 1) * H, :]) for j in range(len(block.offsets)))
        )
        for s in seqs:
            for j in range(len(block.offsets)):
                part = nn(
                    refs.weights[CONV][j * H : (j + 1) * H, :], taps[j * H : (j + 1) * H, self.lanes_of(s)]
                )
                broad[0:H, :] = broad[0:H, :] + part if j else part

            def store(rows, t, value, s=s):
                v[rows, self.lanes_of(s, t)] = value.astype(BF16)

            self.act_back(block, P_NORM, s, H, store)
            self.tick()
        self.norm_grads(block, P_NORM, H)
        value = nt(u[...], v[...])
        self.tick()
        self.give_rows(base + FIRST, [value[0:H], value[H : 2 * H]])
        if ready is not None:
            ready()
        for s in seqs:
            broad[...] = nn(refs.weights[FIRST][...], v[:, self.lanes_of(s)])
            self.act_back(block, OUTER, s, self.plan.width, functools.partial(finish, s))
            self.tick()
        self.norm_grads(block, OUTER, self.plan.width)
        self.reduce(block)

    def x_in(self, block, rows, lanes):
        if block is ENCODER:
            return self.s.given[rows, lanes].astype(F32)
        return self.s.total[rows, lanes]

    def load(self, source):
        self.loading = [
            pltpu.make_async_copy(source.at[s], self.s.given.at[:, self.lanes_of(s)], self.s.local_sem.at[8 + s])
            for s in range(self.plan.seqs)
        ]
        for copy in self.loading:
            copy.start()

    def loaded(self):
        for copy in self.loading:
            copy.wait()

    def run(self):
        plan = self.plan
        self.signal_entry()
        self.load(self.ins.tokens)
        for shard, held in zip(self.ins.shards, self.s.held):
            full, rest = divmod(shard.shape[0], LANES)
            held[self.own + (slice(0, full), slice(None))] = shard[0 : full * LANES].reshape(full, LANES)
            if rest:
                held[self.own + (slice(full, full + 1), slice(0, rest))] = shard[full * LANES :].reshape(1, rest)
        self.wait_entry()
        self.open_gathers()
        for _ in range(LAG + 1):
            self.gather_step()
        for block in BLOCKS:
            self.s.blocks[block.index].sums[...] = jnp.zeros((8, plan.width), F32)
        self.norm_columns()
        self.loaded()
        for s in range(plan.seqs):
            self.act(
                ENCODER,
                OUTER,
                s,
                plan.width,
                lambda rows, t, fresh=False: self.s.given[rows, self.lanes_of(s, t)].astype(F32),
            )
            self.gather_step()
        self.documents()
        self.forward()
        for gather in self.gathers:
            gather.leave()
        self.loaded()
        total, given, dq = self.s.total, self.s.given, self.s.blocks[1].acts[OUTER].value

        def finish_dec(s, rows, t, back):
            lanes = self.lanes_of(s, t)
            value = given[rows, lanes].astype(F32) + back
            total[rows, lanes] = value
            dq[rows, lanes] = value.astype(BF16)

        def finish_enc(s, rows, t, back):
            lanes = self.lanes_of(s, t)
            total[rows, lanes] = total[rows, lanes] + back

        self.backward(DECODER, given, finish_dec)
        self.load(self.ins.tokens)
        self.backward(ENCODER, dq, finish_enc, self.loaded)
        stores = [
            pltpu.make_async_copy(total.at[:, self.lanes_of(s)], self.outs.grad_tokens.at[s], self.s.local_sem.at[8 + s])
            for s in range(plan.seqs)
        ]
        for copy in stores:
            copy.start()
        while self.in_flight:
            self.tick()
        for item in self.scatters + self.reduces:
            item.leave()
        for copy in stores + [self.storing]:
            copy.wait()
        for block, item in zip((DECODER, ENCODER), self.reduces):
            base = plan.small_at[6 + block.index]
            for tile in range(plan.norm_tiles):
                begin, size = tile_span(tile, plan.width)
                self.outs.small[base + 8 * tile : base + 8 * tile + 8, 0:size] = item.result[:, begin : begin + size]


def per_device(
    grid,
    tokens,
    cotangent,
    doc_starts,
    enc_first,
    enc_conv,
    enc_last,
    enc_norm_first,
    enc_norm_inner,
    dec_first,
    dec_conv,
    dec_last,
    dec_norm_first,
    dec_norm_inner,
):
    seqs, seg, width = tokens.shape
    weights = (enc_first, enc_conv, enc_last, dec_first, dec_conv, dec_last)
    norms = [enc_norm_first, enc_norm_inner, dec_norm_first, dec_norm_inner]
    plan = Plan(grid, seqs, seg, width, [w.shape[0] for w in weights])
    vmem = pl.BlockSpec(memory_space=pltpu.VMEM)
    hbm = pl.BlockSpec(memory_space=pl.ANY)
    smem = pl.BlockSpec(memory_space=pltpu.SMEM)
    ins = dict(
        doc_starts=doc_starts,
        tokens=jnp.swapaxes(tokens, 1, 2),
        cotangent=jnp.swapaxes(cotangent, 1, 2),
        shards=list(weights),
        norms=norms,
    )
    in_specs = dict(doc_starts=smem, tokens=hbm, cotangent=hbm, shards=[vmem] * 6, norms=[vmem] * 4)
    shape = jax.ShapeDtypeStruct
    outs = dict(
        out=shape((seqs, width, seg), BF16),
        grad_tokens=shape((seqs, width, seg), F32),
        small=shape((plan.small_at[-1], LANES), F32),
    )
    out_specs = dict(out=hbm, grad_tokens=hbm, small=vmem)
    trees = [jax.tree.structure(tree) for tree in (ins, outs, plan.scratch)]

    def body(*refs):
        named = []
        for tree in trees:
            named.append(spaces(jax.tree.unflatten(tree, refs[: tree.num_leaves])))
            refs = refs[tree.num_leaves :]
        Kernel(plan, *named).run()

    results = pl.pallas_call(
        body,
        out_shape=jax.tree.leaves(outs),
        in_specs=jax.tree.leaves(in_specs),
        out_specs=jax.tree.leaves(out_specs),
        scratch_shapes=jax.tree.leaves(plan.scratch),
        compiler_params=pltpu.CompilerParams(
            collective_id=0, has_side_effects=True, vmem_limit_bytes=64 * 1024 * 1024 - 65536
        ),
    )(*jax.tree.leaves(ins))
    result = spaces(jax.tree.unflatten(trees[1], results))
    parts = hand_over(plan, result.small, weights, norms)
    out, grad_tokens = jnp.swapaxes(result.out, 1, 2), jnp.swapaxes(result.grad_tokens, 1, 2)
    return (out, grad_tokens, *parts[:3], *parts[6:8], *parts[3:6], *parts[8:])


def hand_over(plan, small, weights, norms):
    def body(small, *outs):
        for out, begin in zip(outs[:6], plan.small_at):
            full, rest = divmod(out.shape[0], LANES)
            out[0 : full * LANES] = small[begin : begin + full].reshape(full * LANES)
            if rest:
                out[full * LANES :] = small[begin + full, 0:rest]
        for k, out in enumerate(outs[6:]):
            begin = plan.small_at[6 + k // 2] + 2 * (k % 2)
            count, width = out.shape
            for tile in range(-(-width // LANES)):
                low, size = tile_span(tile, width)
                out[:, low : low + size] = small[begin + 8 * tile : begin + 8 * tile + count, 0:size]

    return pl.pallas_call(
        body, out_shape=[jax.ShapeDtypeStruct(value.shape, F32) for value in (*weights, *norms)]
    )(small)


def solution(mesh):
    flat = P(("batch", "seq"))
    rows = P("batch", "seq", None)
    in_specs = (rows, rows, P("batch", None), flat, flat, flat, P(), P(), flat, flat, flat, P(), P())
    out_specs = (rows, rows, flat, flat, flat, P(), P(), flat, flat, flat, P(), P())
    return jax.shard_map(
        functools.partial(per_device, Grid(mesh)),
        mesh=mesh,
        in_specs=in_specs,
        out_specs=out_specs,
        check_vma=False,
    )
```

```python
import functools
import types

import jax
import jax.numpy as jnp
from jax import lax
from jax.experimental import pallas as pl
from jax.experimental.pallas import tpu as pltpu
from jax.sharding import PartitionSpec as P

H = 400
ENCODER_TAPS = 5
ENCODER_DILATION = 4
DECODER_TAPS = 3
DECODER_DILATION = 16

F32, BF16 = jnp.float32, jnp.bfloat16
MESH = pl.DeviceIdType.MESH
LANES = 128
TILES = 4
CHUNK = 16
REACH = 32
SHARE = 112
SLACK = 8
EPS = 1e-5
HI, LO, CORE, SEQ = 0, 1, 2, 3
ORDER_A = (HI, LO, SEQ, CORE)
ORDER_C = (SEQ, HI, LO, CORE)
LAG = 1
PACE = 2.2
UNROLL = 12
STEP, STEP_UNROLL = 80, 4


def round_up(value, step):
    return -(-value // step) * step


class Grid:
    def __init__(self, mesh):
        batch, seq = mesh.shape["batch"], mesh.shape["seq"]
        lo = 2 if batch <= 16 else 4
        self.sizes = (batch // (2 * lo), lo, 2, seq)
        self.count = batch * seq

    def own(self):
        batch = lax.axis_index("batch")
        lo = self.sizes[1]
        return (batch // (2 * lo), (batch // 2) % lo, batch % 2, lax.axis_index("seq"))

    def device(self, place):
        hi, lo, core, seq = place
        return ((hi * self.sizes[1] + lo) * 2 + core, seq)

    def peer(self, own, dim, distance):
        place = list(own)
        place[dim] = lax.rem(own[dim] + distance, self.sizes[dim])
        return tuple(place)

    def slot(self, dim, distance):
        return sum(size - 1 for size in self.sizes[:dim]) + distance - 1

    def slots(self):
        return sum(size - 1 for size in self.sizes)


def split_rows(rows):
    first = round_up(int(rows * 0.6), 16)
    parts = [(0, first, ORDER_A)]
    if first < rows:
        parts.append((first, rows - first, ORDER_C))
    return parts


def remote(source, target, send, receive, device):
    copy = pltpu.make_async_remote_copy(
        source, target, send, receive, device_id=device, device_id_type=MESH
    )
    copy.start()
    return copy


class Gather:
    def __init__(self, grid, own, held, send, receive, rows):
        self.grid, self.own, self.held = grid, own, held
        self.send, self.receive = send, receive
        self.parts = split_rows(rows)
        self.copies = {}

    def start(self, stage):
        for color, (begin, count, order) in enumerate(self.parts):
            dim, done = order[stage], order[:stage]
            index = tuple(slice(None) if d in done else self.own[d] for d in range(4))
            block = self.held.at[index + (pl.ds(begin, count),)]
            copies = []
            for distance in range(1, self.grid.sizes[dim]):
                slot = self.grid.slot(dim, distance)
                target = self.grid.device(self.grid.peer(self.own, dim, distance))
                copies.append(
                    remote(
                        block,
                        block,
                        self.send.at[color, slot],
                        self.receive.at[color, slot],
                        target,
                    )
                )
            self.copies[color, stage] = copies

    def arrive(self, stage):
        for color in range(len(self.parts)):
            for copy in self.copies[color, stage]:
                copy.wait_recv()

    def leave(self):
        for copies in self.copies.values():
            for copy in copies:
                copy.wait_send()


def landing_shapes(grid, rows):
    shapes = []
    for begin, count, order in split_rows(rows):
        back = order[::-1]
        for stage, dim in enumerate(back):
            rest = tuple(grid.sizes[d] for d in range(4) if d not in back[: stage + 1])
            shapes.append((grid.sizes[dim] - 1,) + rest + (count, LANES))
    return shapes


class Scatter:
    def __init__(self, grid, own, held, landing, send, receive, rows, result):
        self.grid, self.own, self.held, self.landing = grid, own, held, landing
        self.send, self.receive, self.result = send, receive, result
        self.parts = split_rows(rows)
        self.copies = {}
        self.stage = 0

    def start(self):
        for color, (begin, count, order) in enumerate(self.parts):
            back = order[::-1]
            dim, done = back[self.stage], back[: self.stage]
            copies = []
            for distance in range(1, self.grid.sizes[dim]):
                place = self.grid.peer(self.own, dim, distance)
                index = tuple(
                    self.own[d] if d in done else place[d] if d == dim else slice(None)
                    for d in range(4)
                )
                slot = self.grid.slot(dim, distance)
                copies.append(
                    remote(
                        self.held.at[index + (pl.ds(begin, count),)],
                        self.landing[color * 4 + self.stage].at[distance - 1],
                        self.send.at[color, slot],
                        self.receive.at[color, slot],
                        self.grid.device(place),
                    )
                )
            self.copies[color, self.stage] = copies

    def finish(self):
        for color, (begin, count, order) in enumerate(self.parts):
            back = order[::-1]
            done = back[: self.stage + 1]
            rest = [d for d in range(4) if d not in done]
            for copy in self.copies[color, self.stage]:
                copy.wait_recv()
            landing = self.landing[color * 4 + self.stage]
            senders = landing.shape[0]
            blocks = 1
            for d in rest:
                blocks *= self.grid.sizes[d]

            def add(block, carry, begin=begin, count=count, landing=landing, rest=rest):
                left, place = block, {}
                for d in reversed(rest):
                    place[d] = left % self.grid.sizes[d]
                    left = left // self.grid.sizes[d]
                index = tuple(place.get(d, self.own[d]) for d in range(4))
                total = self.held[index + (pl.ds(begin, count),)].astype(F32)
                for sender in range(senders):
                    where = (sender,) + tuple(place[d] for d in rest)
                    total = total + landing[where].astype(F32)
                if rest:
                    self.held[index + (pl.ds(begin, count),)] = total.astype(BF16)
                else:
                    self.result[pl.ds(begin, count), :] = total
                return carry

            if blocks == 1:
                add(0, 0)
            else:
                lax.fori_loop(0, blocks, add, 0, unroll=2 if blocks % 2 == 0 else 1)
        self.stage += 1

    def leave(self):
        for copies in self.copies.values():
            for copy in copies:
                copy.wait_send()


class Reduce:
    ORDER = (CORE, SEQ, LO, HI)

    def __init__(self, grid, own, slots, send, receive):
        self.grid, self.own, self.slots = grid, own, slots
        self.send, self.receive = send, receive
        self.copies = {}
        self.stage = 0

    def start(self, value=None):
        dim = self.ORDER[self.stage]
        slots, mine = self.slots[dim], self.own[dim]
        if value is not None:
            slots[mine] = value
        self.copies[self.stage] = [
            remote(
                slots.at[mine],
                slots.at[mine],
                self.send.at[self.grid.slot(dim, distance)],
                self.receive.at[self.grid.slot(dim, distance)],
                self.grid.device(self.grid.peer(self.own, dim, distance)),
            )
            for distance in range(1, self.grid.sizes[dim])
        ]

    def finish(self):
        dim = self.ORDER[self.stage]
        for copy in self.copies[self.stage]:
            copy.wait_recv()
        total = self.slots[dim][0]
        for other in range(1, self.grid.sizes[dim]):
            total = total + self.slots[dim][other]
        self.stage += 1
        if self.stage < 4:
            following = self.ORDER[self.stage]
            self.slots[following][self.own[following]] = total
        else:
            self.result = total

    def leave(self):
        for copies in self.copies.values():
            for copy in copies:
                copy.wait_send()


def lane_ids(rows):
    return lax.broadcasted_iota(jnp.int32, (rows, LANES), 1)


def period_of(elements):
    group = 1
    while (group * elements) % H:
        group *= 2
    return group


class Pieces:
    def __init__(self, grid, elements):
        self.grid, self.elements = grid, elements
        self.rows = round_up(-(-elements // LANES), 16)
        self.pitch = self.rows + SLACK
        self.group = period_of(elements)
        self.groups = grid.count // self.group
        self.period = self.group * elements // H
        self.passes = 2 if self.groups % 16 == 0 else 1
        self.matrix_rows = grid.count * elements // H
        self.part_rows = self.matrix_rows // self.passes

    def flat_rows(self):
        return self.grid.count // self.passes * self.pitch + SLACK

    def each(self, held, flat, part, widen):
        _, lo, core, seq = self.grid.sizes
        count = self.grid.count // self.passes

        def body(local, carry):
            piece = local + part * count
            index = (piece // (lo * core * seq), (piece // (core * seq)) % lo, (piece // seq) % core, piece % seq)
            begin = pl.multiple_of(local * self.pitch + SLACK, SLACK)
            if widen:
                flat[pl.ds(begin, self.rows), :] = held[index].astype(F32)
            else:
                held[index] = flat[pl.ds(begin, self.rows), :].astype(BF16)
            return carry

        lax.fori_loop(0, count, body, 0, unroll=4)

    def at(self, piece, row):
        count = self.groups // self.passes
        return (pl.ds(piece * self.pitch + row, count, stride=self.group * self.pitch), slice(None))

    def row_at(self, row, lead=0):
        count = self.groups // self.passes
        return (pl.ds(row + lead, count, stride=self.period), slice(None))

    def unpack(self, held, flat, matrix, part, lead):
        lane = lane_ids(self.groups // self.passes)
        self.each(held, flat, part, True)
        for piece in range(self.group):
            offset = piece * self.elements
            first, last = -(-offset // H), (offset + self.elements) // H

            def body(row, carry, piece=piece, offset=offset):
                local = row * H - offset + SLACK * LANES
                source, shift = local // LANES, local % LANES
                keep = lane < LANES - shift
                back = lax.rem(LANES - shift, LANES)
                rolled = [
                    pltpu.roll(flat[self.at(piece, source + t)], back, axis=1)
                    for t in range(TILES + 1)
                ]
                for tile in range(TILES):
                    matrix.at[tile][self.row_at(row, lead)] = jnp.where(
                        keep, rolled[tile], rolled[tile + 1]
                    )
                return carry

            if last > first:
                lax.fori_loop(first, last, body, 0, unroll=last - first)
            if (offset + self.elements) % H:
                self.shared_row(flat, matrix, piece, last, lane, lead)

    def shared_row(self, flat, matrix, piece, row, lane, lead):
        local = row * H - piece * self.elements
        cut = (piece + 1) * self.elements - row * H
        for tile in range(TILES):
            begin, end = tile * LANES, min((tile + 1) * LANES, H)
            value = jnp.zeros(lane.shape, F32)
            position = begin
            while position < end:
                if position < cut:
                    owner, at, stop = piece, local + position, min(end, cut)
                else:
                    owner, at, stop = piece + 1, position - cut, end
                source, slot = at // LANES + SLACK, at % LANES
                stop = min(stop, position + LANES - slot)
                goal = position - begin
                rolled = pltpu.roll(flat[self.at(owner, source)], (goal - slot) % LANES, axis=1)
                value = jnp.where((lane >= goal) & (lane < goal + stop - position), rolled, value)
                position = stop
            matrix.at[tile][self.row_at(row, lead)] = value

    def pack(self, matrix, flat, held, part):
        lane = lane_ids(self.groups // self.passes)
        for piece in range(self.group):
            offset = piece * self.elements
            first, last = offset // H, -(-(offset + self.elements) // H)

            def body(row, pending, piece=piece, offset=offset):
                local = row * H - offset + SLACK * LANES
                target, shift = local // LANES, local % LANES
                keep = lane >= shift
                rolled = [
                    pltpu.roll(matrix.at[tile][self.row_at(row)], shift, axis=1) for tile in range(TILES)
                ]
                before = pending
                for tile in range(TILES):
                    value = jnp.where(keep, rolled[tile], before)
                    flat[self.at(piece, target + tile)] = value
                    before = rolled[tile]
                return jnp.where(shift + H % LANES > LANES, rolled[-1], value)

            pending = lax.fori_loop(first, last, body, jnp.zeros(lane.shape, F32), unroll=last - first)
            ending = (last * H - offset + SLACK * LANES) // LANES
            flat[self.at(piece, ending)] = pending
        self.each(held, flat, part, False)


def dot(a, b, left, right, precision=None):
    return lax.dot_general(
        a, b, (((left,), (right,)), ((), ())), precision=precision, preferred_element_type=F32
    )


def nn(a, b):
    return dot(a, b, 1, 0)


def nt(a, b):
    return dot(a, b, 1, 1)


def tn(a, b):
    return dot(a, b, 0, 0)


def tile_span(tile, width):
    return tile * LANES, min(LANES, width - tile * LANES)


def chunks(count, body, carry=0):
    def step(index, carry):
        return body(pl.multiple_of(index * CHUNK, CHUNK), carry)

    return lax.fori_loop(0, count // CHUNK, step, carry, unroll=UNROLL)


def steps(count, body, carry=0):
    def step(index, carry):
        return body(pl.multiple_of(index * STEP, CHUNK), carry)

    return lax.fori_loop(0, count // STEP, step, carry, unroll=STEP_UNROLL)


def fold(value):
    total = value[0:CHUNK]
    for begin in range(CHUNK, value.shape[0], CHUNK):
        total = total + value[begin : begin + CHUNK]
    return total


def zeros(tiles):
    return (jnp.zeros((CHUNK, LANES), F32),) * tiles


def column_sums(totals, count):
    return [jnp.sum(total, axis=0, keepdims=True) * (1.0 / count) for total in totals]


def gelu_parts(a):
    bell = jnp.exp(a * a * -0.5)
    t = 1.0 / (1.0 + jnp.abs(a) * (0.3275911 * 0.7071067811865476))
    poly = 1.061405429 * t - 1.453152027
    poly = ((poly * t + 1.421413741) * t - 0.284496736) * t + 0.254829592
    tail = poly * t * bell * 0.5
    phi = jnp.where(a >= 0.0, 1.0 - tail, tail)
    return a * phi, phi + a * bell * 0.3989422804014327


class Block:
    def __init__(self, index, offsets, norms):
        self.index, self.offsets = index, offsets
        self.before, self.after = min(offsets) < 0, max(offsets) > 0
        self.norms = norms


ENCODER = Block(
    0, [(j - ENCODER_TAPS // 2) * ENCODER_DILATION for j in range(ENCODER_TAPS)], (0, 1)
)
DECODER = Block(1, [(j - DECODER_TAPS + 1) * DECODER_DILATION for j in range(DECODER_TAPS)], (2, 3))
BLOCKS = (ENCODER, DECODER)
FIRST, CONV, LAST = 0, 1, 2
OUTER, P_NORM, C_NORM = 0, 1, 2


def spaces(tree):
    if isinstance(tree, dict):
        return types.SimpleNamespace(**{key: spaces(value) for key, value in tree.items()})
    if isinstance(tree, (list, tuple)):
        return [spaces(value) for value in tree]
    return tree


class Plan:
    def __init__(self, grid, seqs, seg, width, elements):
        self.grid, self.seqs, self.seg, self.width = grid, seqs, seg, width
        self.rows = seqs * seg
        self.tiles = seg // LANES
        self.pieces = [Pieces(grid, count) for count in elements]
        self.norm_tiles = -(-width // LANES)
        sizes = [p.rows for p in self.pieces] + [8 * self.norm_tiles] * 2
        self.small_at = [sum(sizes[:k]) for k in range(len(sizes) + 1)]
        vmem, dma = pltpu.VMEM, pltpu.SemaphoreType.DMA
        rows, count = self.rows, len(elements)

        def block(which):
            taps = len(which.offsets)
            half = dict(
                normed=vmem((H, rows), BF16), slope=vmem((H, rows), BF16), value=vmem((H, rows), BF16)
            )
            return dict(
                weights=[vmem((width, H), BF16), vmem((taps * H, H), BF16), vmem((H, width), BF16)],
                acts=[dict(slope=vmem((width, rows), BF16), value=vmem((width, rows), BF16)), half, half],
                halo=[[vmem((2, seqs, SHARE, LANES), BF16) for _ in range(2)] for _ in range(2)],
                stats=vmem((8, rows), F32),
                outer=vmem((2, width, LANES), F32),
                inner=vmem((4, H, LANES), F32),
                sums=vmem((8, width), F32),
                slots=[vmem((size, 8, width), F32) for size in grid.sizes],
            )

        self.scratch = dict(
            held=[vmem(grid.sizes + (p.rows, LANES), BF16) for p in self.pieces],
            landing=[[vmem(shape, BF16) for shape in landing_shapes(grid, p.rows)] for p in self.pieces],
            flat=vmem((max(p.flat_rows() for p in self.pieces), LANES), F32),
            matrix=vmem((TILES, max(p.part_rows for p in self.pieces) + 16, LANES), F32),
            blocks=[block(which) for which in BLOCKS],
            given=vmem((width, rows), BF16),
            total=vmem((width, rows), F32),
            staged=vmem((width, seg), BF16),
            wide=vmem((seqs, H, seg + 2 * LANES), BF16),
            begin=vmem((seqs, CHUNK, seg + 2 * LANES), jnp.int32),
            taps=vmem((ENCODER_TAPS * H, rows), BF16),
            broad=vmem((width, rows), F32),
            spread=vmem((2, width, LANES), F32),
            local_sem=dma((count + 2 * seqs + 2,)),
            gather_sem=dma((2, count, 2, grid.slots())),
            scatter_sem=dma((2, count, 2, grid.slots())),
            reduce_sem=dma((2, 2, grid.slots())),
            halo_sem=dma((2, 4, seqs, 2)),
        )


class Kernel:
    def __init__(self, plan, ins, outs, scratch):
        self.plan, self.grid, self.own = plan, plan.grid, plan.grid.own()
        self.ins, self.outs, self.s = ins, outs, scratch
        self.in_flight, self.scatters, self.reduces = [], [], []
        self.clock = 0.0


    def signal_entry(self):
        barrier = pltpu.get_barrier_semaphore()
        for dim in range(4):
            for distance in range(1, self.grid.sizes[dim]):
                pl.semaphore_signal(
                    barrier,
                    inc=1,
                    device_id=self.grid.device(self.grid.peer(self.own, dim, distance)),
                    device_id_type=MESH,
                )

    def wait_entry(self):
        pl.semaphore_wait(pltpu.get_barrier_semaphore(), self.grid.slots())

    def open_gathers(self):
        self.gathers = [
            Gather(
                self.grid,
                self.own,
                self.s.held[k],
                self.s.gather_sem.at[0, k],
                self.s.gather_sem.at[1, k],
                pieces.rows,
            )
            for k, pieces in enumerate(self.plan.pieces)
        ]
        self.step, self.arrived = 0, set()

    def gather_step(self):
        t, count = self.step, len(self.gathers)
        if t >= count + 4 * LAG:
            return
        for stage in reversed(range(4)):
            k = t - LAG * (stage + 1)
            if 0 <= k < count:
                if stage < 3 or k not in self.arrived:
                    self.gathers[k].arrive(stage)
                if stage < 3:
                    self.gathers[k].start(stage + 1)
        if t < count:
            self.gathers[t].start(0)
        self.step += 1

    def gather_until(self, k):
        while self.step < k + 4 * LAG:
            self.gather_step()
        if k not in self.arrived and self.step == k + 4 * LAG:
            self.gathers[k].arrive(3)
            self.arrived.add(k)

    def tick(self, spent=None):
        self.clock += spent or 0.0
        for item in list(self.in_flight):
            if spent is None or self.clock - item.began >= item.wait[item.stage]:
                item.finish()
                if item.stage < 4:
                    self.begin(item)
                else:
                    self.in_flight.remove(item)

    def begin(self, item, *first):
        item.start(*first)
        item.began = self.clock

    def scatter(self, k):
        item = Scatter(
            self.grid,
            self.own,
            self.s.held[k],
            self.s.landing[k],
            self.s.scatter_sem.at[0, k],
            self.s.scatter_sem.at[1, k],
            self.plan.pieces[k].rows,
            self.outs.small.at[pl.ds(self.plan.small_at[k], self.plan.pieces[k].rows)],
        )
        per_row = self.plan.pieces[k].rows * 0.01
        item.wait = [PACE * (1.5 + per_row)] + [PACE * (3.0 + 2 * per_row)] * 3
        self.begin(item)
        self.in_flight.append(item)
        self.scatters.append(item)

    def reduce(self, block):
        k, refs = block.index, self.s.blocks[block.index]
        item = Reduce(
            self.grid, self.own, refs.slots, self.s.reduce_sem.at[0, k], self.s.reduce_sem.at[1, k]
        )
        item.wait = [1.5, 3.0, 3.0, 3.0]
        self.begin(item, refs.sums[...])
        self.in_flight.append(item)
        self.reduces.append(item)

    def send_halo(self, block, way, s):
        seg, size, way_refs = self.plan.seg, self.grid.sizes[SEQ], self.s.blocks[block.index].halo[way]
        before, after = (block.after, block.before) if way else (block.before, block.after)
        copies = []
        for side, wanted, begin, distance in ((0, before, seg, 1), (1, after, LANES, size - 1)):
            if wanted:
                phase = 2 * block.index + way
                message = way_refs[side].at[0, s]
                self.pack_halo(s, begin, LANES - REACH if side == 0 else 0, message)
                copy = remote(
                    message,
                    way_refs[side].at[1, s],
                    self.s.halo_sem.at[0, phase, s, side],
                    self.s.halo_sem.at[1, phase, s, side],
                    self.grid.device(self.grid.peer(self.own, SEQ, distance)),
                )
                copies.append((side, copy))
        return copies

    def shares(self):
        return [(quarter, begin, min(SHARE, H - begin)) for quarter, begin in enumerate(range(0, H, SHARE))]

    def pack_halo(self, s, begin, lane, message):
        lanes = lane_ids(SHARE)
        total = jnp.zeros((SHARE, LANES), F32)
        for quarter, row, rows in self.shares():
            value = self.s.wide[s, row : row + rows, begin : begin + LANES].astype(F32)
            if rows < SHARE:
                value = jnp.concatenate([value, jnp.zeros((SHARE - rows, LANES), F32)], axis=0)
            value = pltpu.roll(value, (quarter * REACH - lane) % LANES, axis=1)
            total = jnp.where(lanes >= quarter * REACH, value, total)
        message[...] = total.astype(BF16)

    def take_halo(self, block, way, s, copies):
        for side, copy in copies:
            copy.wait()
            begin = (self.plan.seg + LANES) if side else 0
            lane = 0 if side else LANES - REACH
            message = self.s.blocks[block.index].halo[way][side][1, s].astype(F32)
            for quarter, row, rows in self.shares():
                value = pltpu.roll(message, (lane - quarter * REACH) % LANES, axis=1)
                self.s.wide[s, row : row + rows, begin : begin + LANES] = value[0:rows].astype(BF16)


    def unpack(self, k):
        self.gather_until(k)
        pieces, matrix, step = self.plan.pieces[k], self.s.matrix, 32 if k % 3 == LAST else 16
        lead = 0
        for part in range(pieces.passes):
            pieces.unpack(self.s.held[k], self.s.flat, matrix, part, lead)
            ready = (lead + pieces.part_rows) // step * step
            self.convert(k, part * pieces.part_rows - lead, ready)
            lead = lead + pieces.part_rows - ready
            if lead:
                matrix[:, 0:lead, :] = matrix[:, ready : ready + lead, :]

    def convert(self, k, base, rows):
        target = self.s.blocks[k // 3].weights[k % 3]
        matrix, chunk = self.s.matrix, 16
        if k % 3 == LAST:
            keep = lane_ids(chunk) < H % LANES

            def body(index, carry):
                r = pl.multiple_of(index * chunk, 16)
                left = [matrix.at[c][pl.ds(2 * r, chunk, stride=2), :] for c in range(TILES)]
                right = [
                    pltpu.roll(matrix.at[c][pl.ds(2 * r + 1, chunk, stride=2), :], H % LANES, axis=1)
                    for c in range(TILES)
                ]
                tiles = left[:3] + [jnp.where(keep, left[3], right[0])]
                tiles += [jnp.where(keep, right[c], right[c + 1]) for c in range(3)]
                for c, value in enumerate(tiles):
                    begin, size = tile_span(c, target.shape[1])
                    goal = pl.multiple_of(base // 2 + r, 16)
                    target[pl.ds(goal, chunk), begin : begin + size] = value[:, :size].astype(BF16)
                return carry

            lax.fori_loop(0, rows // (2 * chunk), body, 0, unroll=4)
        else:

            def body(index, carry):
                r = pl.multiple_of(index * chunk, 16)
                goal = pl.multiple_of(base + r, 16)
                for c in range(TILES):
                    begin, size = tile_span(c, H)
                    target[pl.ds(goal, chunk), begin : begin + size] = matrix[c, pl.ds(r, chunk), :size].astype(BF16)
                return carry

            lax.fori_loop(0, rows // chunk, body, 0, unroll=4)

    def give(self, k, part):
        pieces = self.plan.pieces[k]
        pieces.pack(self.s.matrix, self.s.flat, self.s.held[k], part)
        if part == pieces.passes - 1:
            self.scatter(k)

    def grad_rows(self, begin, value):
        for c in range(TILES):
            low, size = tile_span(c, H)
            self.s.matrix[c, begin : begin + value.shape[0], 0:size] = value[:, low : low + size]

    def give_rows(self, k, values):
        pieces, broad = self.plan.pieces[k], self.s.broad
        part, room = 0, pieces.part_rows
        for value in values:
            begin = 0
            while begin < H:
                count = min(room, H - begin)
                if begin:
                    self.grad_rows(pieces.part_rows - room, broad[0:count, 0:H])
                else:
                    self.grad_rows(pieces.part_rows - room, value[0:count])
                    if count < H:
                        broad[0 : H - count, 0:H] = value[count:]
                begin, room = begin + count, room - count
                if not room:
                    self.give(k, part)
                    self.tick(1.0)
                    part, room = part + 1, pieces.part_rows
            self.tick(1.0)

    def give_last(self, k, value):
        width, matrix, chunk = self.plan.width, self.s.matrix, 40
        pieces, store = self.plan.pieces[k], self.s.broad
        tiles_of = -(-width // LANES)
        store[0:H, 0:width] = value
        keep = lane_ids(chunk) < LANES - H % LANES
        for part in range(pieces.passes):
            base = part * pieces.part_rows // 2

            def body(index, carry, base=base):
                r = pl.multiple_of(index * chunk, 8)
                rows = pl.ds(pl.multiple_of(base + r, 8), chunk)
                tiles = [store[rows, c * LANES : (c + 1) * LANES] for c in range(tiles_of)]
                for c in range(TILES):
                    matrix.at[c][pl.ds(2 * r, chunk, stride=2), :] = tiles[c]
                back = [pltpu.roll(value, LANES - H % LANES, axis=1) for value in tiles[3:]]
                back.append(back[-1])
                for c in range(TILES):
                    matrix.at[c][pl.ds(2 * r + 1, chunk, stride=2), :] = jnp.where(keep, back[c], back[c + 1])
                return carry

            lax.fori_loop(0, pieces.part_rows // (2 * chunk), body, 0)
            self.give(k, part)


    def documents(self):
        seg, span = self.plan.seg, self.plan.seg + 2 * LANES
        whole = seg * self.grid.sizes[SEQ]
        place = lax.broadcasted_iota(jnp.int32, (CHUNK, span), 1) + (self.own[SEQ] * seg - LANES)
        for s in range(self.plan.seqs):
            begin = jnp.zeros((CHUNK, span), jnp.int32)
            for k in range(self.ins.doc_starts.shape[1]):
                head = self.ins.doc_starts[s, k]
                begin = jnp.maximum(begin, jnp.where(place >= head, head, 0))
            begin = jnp.where(place < 0, -1, begin)
            self.s.begin[s] = jnp.where(place >= whole, -2, begin)

    def shifted(self, tiles, shift, lane):
        count = len(tiles) - 2
        if not shift:
            return tiles[1:-1]
        rolled = [pltpu.roll(tile, -shift % LANES, axis=1) for tile in tiles]
        if shift > 0:
            return [jnp.where(lane < LANES - shift, rolled[c + 1], rolled[c + 2]) for c in range(count)]
        return [jnp.where(lane >= -shift, rolled[c + 1], rolled[c]) for c in range(count)]

    def spread_taps(self, block, s, sign):
        count, seg, wide, taps = self.plan.tiles, self.plan.seg, self.s.wide, self.s.taps
        lane = lane_ids(CHUNK)
        heads = [self.s.begin[s, :, t * LANES : (t + 1) * LANES] for t in range(count + 2)]
        inside = [
            [there == here for there, here in zip(self.shifted(heads, sign * offset, lane), heads[1:-1])]
            for offset in block.offsets
        ]

        def body(r, carry):
            tiles = [wide[s, pl.ds(r, CHUNK), t * LANES : (t + 1) * LANES].astype(F32) for t in range(count + 2)]
            for j, offset in enumerate(block.offsets):
                for t, value in enumerate(self.shifted(tiles, sign * offset, lane)):
                    if offset:
                        value = jnp.where(inside[j][t], value, 0.0)
                    begin = s * seg + t * LANES
                    taps[pl.ds(pl.multiple_of(j * H + r, CHUNK), CHUNK), begin : begin + LANES] = value.astype(BF16)
            return carry

        chunks(H, body)


    def norm_columns(self):
        for block in BLOCKS:
            refs = self.s.blocks[block.index]
            for source, target in zip(block.norms, (refs.outer, refs.inner)):
                rows = self.ins.norms[source]
                for k in range(rows.shape[0]):
                    for tile in range(-(-rows.shape[1] // LANES)):
                        begin, size = tile_span(tile, rows.shape[1])
                        row = rows[k : k + 1, begin : begin + size]
                        target[k, begin : begin + size, :] = jnp.broadcast_to(row, (LANES, size)).T

    def gains(self, block, norm):
        refs = self.s.blocks[block.index]
        if norm == OUTER:
            return refs.outer.at[0], refs.outer.at[1]
        return refs.inner.at[2 * norm - 2], refs.inner.at[2 * norm - 1]

    def lanes_of(self, s, t=None):
        if t is None:
            return slice(s * self.plan.seg, (s + 1) * self.plan.seg)
        begin = s * self.plan.seg + t * LANES
        return slice(begin, begin + LANES)

    def act(self, block, norm, s, count, load, wide=False):
        tiles = range(self.plan.tiles)
        refs = self.s.blocks[block.index]
        act, stats = refs.acts[norm], refs.stats
        gain, shift = self.gains(block, norm)

        def first(r, carry):
            rows = pl.ds(r, STEP)
            return tuple(carry[t] + fold(load(rows, t, True)) for t in tiles)

        centre = column_sums(steps(count, first, zeros(len(tiles))), count)

        def second(r, carry):
            rows, out = pl.ds(r, STEP), []
            for t in tiles:
                away = load(rows, t) - centre[t]
                out.append(carry[t] + fold(away * away))
            return tuple(out)

        spread = column_sums(steps(count, second, zeros(len(tiles))), count)
        scale = [lax.rsqrt(value + EPS) for value in spread]

        def third(r, carry):
            rows = pl.ds(r, STEP)
            g, b = gain[rows, :], shift[rows, :]
            for t in tiles:
                lanes = self.lanes_of(s, t)
                normed = (load(rows, t) - centre[t]) * scale[t]
                value, slope = gelu_parts(normed * g + b)
                value = value.astype(BF16)
                act.value[rows, lanes] = value
                act.slope[rows, lanes] = slope.astype(BF16)
                if norm != OUTER:
                    act.normed[rows, lanes] = normed.astype(BF16)
                if wide:
                    self.s.wide[s, rows, (t + 1) * LANES : (t + 2) * LANES] = value
            return carry

        steps(count, third)
        for t in tiles:
            lanes = self.lanes_of(s, t)
            if norm == OUTER:
                stats[0:1, lanes] = centre[t]
            stats[norm + 1 : norm + 2, lanes] = scale[t]

    def act_back(self, block, norm, s, count, store, broad):
        tiles = range(self.plan.tiles)
        refs, spread = self.s.blocks[block.index], self.s.spread
        act, stats = refs.acts[norm], refs.stats
        gain, _ = self.gains(block, norm)
        scale = [stats[norm + 1 : norm + 2, self.lanes_of(s, t)] for t in tiles]
        centre = [stats[0:1, self.lanes_of(s, t)] for t in tiles]

        def normed(rows, t):
            if norm == OUTER:
                return (self.x_in(block, rows, self.lanes_of(s, t)) - centre[t]) * scale[t]
            return act.normed[rows, self.lanes_of(s, t)].astype(F32)

        def first(r, carry):
            rows = pl.ds(r, STEP)
            g = gain[rows, :]
            ones, twos = [], []
            for t in tiles:
                e = broad[rows, self.lanes_of(s, t)] * act.slope[rows, self.lanes_of(s, t)].astype(F32)
                n = normed(rows, t)
                en, weighted = e * n, e * g
                ones.append(carry[0][t] + fold(weighted))
                twos.append(carry[1][t] + fold(weighted * n))
                gains, shifts = (gains + en, shifts + e) if t else (en, e)
            if s:
                gains, shifts = gains + spread[0, rows, :], shifts + spread[1, rows, :]
            spread[0, rows, :] = gains
            spread[1, rows, :] = shifts
            return tuple(ones), tuple(twos)

        ones, twos = steps(count, first, (zeros(len(tiles)), zeros(len(tiles))))
        ones, twos = column_sums(ones, count), column_sums(twos, count)

        def second(r, carry):
            rows = pl.ds(r, STEP)
            g = gain[rows, :]
            for t in tiles:
                lanes = self.lanes_of(s, t)
                weighted = broad[rows, lanes] * act.slope[rows, lanes].astype(F32) * g
                store(rows, t, (weighted - ones[t] - normed(rows, t) * twos[t]) * scale[t])
            return carry

        return lambda: steps(count, second)

    def norm_grads(self, block, norm, count):
        sums = self.s.blocks[block.index].sums
        for k in range(2):
            for tile in range(-(-count // LANES)):
                begin, size = tile_span(tile, count)
                block_rows = self.s.spread[k, begin : begin + size, :].T
                sums[2 * norm + k : 2 * norm + k + 1, begin : begin + size] = jnp.sum(
                    block_rows, axis=0, keepdims=True
                )


    def from_broad(self, s):
        return lambda rows, t, again=False: self.s.broad[rows, self.lanes_of(s, t)]

    def forward_inner(self, block):
        refs, broad = self.s.blocks[block.index], self.s.broad
        base, taps = 3 * block.index, len(block.offsets)
        seqs = range(self.plan.seqs)
        self.unpack(base + FIRST)
        halos = []
        broad[0:H, :] = tn(refs.weights[FIRST][...], refs.acts[OUTER].value[...])
        self.gather_step()
        for s in seqs:
            self.act(block, P_NORM, s, H, self.from_broad(s), wide=True)
            halos.append(self.send_halo(block, 0, s))
        self.unpack(base + CONV)
        for s in seqs:
            self.take_halo(block, 0, s, halos[s])
            self.spread_taps(block, s, 1)
        broad[0:H, :] = tn(refs.weights[CONV][...], self.s.taps[0 : taps * H, :])
        self.gather_step()
        for s in seqs:
            self.act(block, C_NORM, s, H, self.from_broad(s))
        self.unpack(base + LAST)

    def forward(self):
        broad, total, plan = self.s.broad, self.s.total, self.plan
        self.forward_inner(ENCODER)
        refs = self.s.blocks[0]
        broad[...] = tn(refs.weights[LAST][...], refs.acts[C_NORM].value[...])
        self.gather_step()
        for s in range(plan.seqs):

            def load(rows, t, fresh=False, s=s):
                lanes = self.lanes_of(s, t)
                if fresh:
                    total[rows, lanes] = self.s.given[rows, lanes].astype(F32) + broad[rows, lanes]
                return total[rows, lanes]

            self.act(DECODER, OUTER, s, plan.width, load)
        self.load(self.ins.cotangent)
        self.forward_inner(DECODER)
        refs = self.s.blocks[1]
        broad[...] = tn(refs.weights[LAST][...], refs.acts[C_NORM].value[...])
        self.gather_step()
        for s in range(plan.seqs):
            if s:
                copy.wait()

            def finish(r, carry, s=s):
                rows = pl.ds(r, CHUNK)
                value = total[rows, self.lanes_of(s)] + broad[rows, self.lanes_of(s)]
                self.s.staged[rows, :] = value.astype(BF16)
                return carry

            chunks(plan.width, finish)
            copy = pltpu.make_async_copy(self.s.staged, self.outs.out.at[s], self.s.local_sem.at[6])
            copy.start()
        self.storing = copy


    def backward(self, block, dq, finish, done, ready=None):
        refs, broad, taps = self.s.blocks[block.index], self.s.broad, self.s.taps
        base, seqs = 3 * block.index, range(self.plan.seqs)
        v, w, u = (refs.acts[k].value for k in (P_NORM, C_NORM, OUTER))
        halos = []
        broad[0:H, :] = nn(refs.weights[LAST][...], dq[...])
        for s in seqs:

            def store(rows, t, value, s=s):
                self.s.wide[s, rows, (t + 1) * LANES : (t + 2) * LANES] = value.astype(BF16)

            self.act_back(block, C_NORM, s, H, store, broad)()
            halos.append(self.send_halo(block, 1, s))
            self.tick(1.5)
        self.norm_grads(block, C_NORM, H)
        self.give_last(base + LAST, nt(w[...], dq[...]))
        self.tick(3.0)
        for s in seqs:
            self.take_halo(block, 1, s, halos[s])
            self.spread_taps(block, s, -1)
            self.tick(1.0)
        self.give_rows(
            base + CONV, (nt(v[...], taps[j * H : (j + 1) * H, :]) for j in range(len(block.offsets)))
        )
        for j in range(len(block.offsets)):
            part = nn(refs.weights[CONV][j * H : (j + 1) * H, :], taps[j * H : (j + 1) * H, :])
            broad[0:H, :] = broad[0:H, :] + part if j else part
            self.tick(1.0)
        for s in seqs:

            def store(rows, t, value, s=s):
                v[rows, self.lanes_of(s, t)] = value.astype(BF16)

            self.act_back(block, P_NORM, s, H, store, broad)()
            self.tick(1.0)
        self.norm_grads(block, P_NORM, H)
        value = nt(u[...], v[...])
        self.give_rows(base + FIRST, [value[0:H], value[H : 2 * H]])
        self.tick(1.5)
        if ready is not None:
            ready()
        rest = []
        broad[...] = nn(refs.weights[FIRST][...], v[...])
        self.tick(1.2)
        for s in seqs:
            store = functools.partial(finish, s)
            rest.append(self.act_back(block, OUTER, s, self.plan.width, store, broad))
            self.tick(1.0)
        self.norm_grads(block, OUTER, self.plan.width)
        self.reduce(block)
        for s in seqs:
            rest[s]()
            done(s)
            self.tick(1.0)

    def x_in(self, block, rows, lanes):
        if block is ENCODER:
            return self.s.given[rows, lanes].astype(F32)
        return self.s.total[rows, lanes]

    def load(self, source):
        self.loading = [
            pltpu.make_async_copy(source.at[s], self.s.given.at[:, self.lanes_of(s)], self.s.local_sem.at[8 + s])
            for s in range(self.plan.seqs)
        ]
        for copy in self.loading:
            copy.start()

    def loaded(self):
        for copy in self.loading:
            copy.wait()

    def run(self):
        plan = self.plan
        self.signal_entry()
        self.load(self.ins.tokens)
        for shard, held in zip(self.ins.shards, self.s.held):
            full, rest = divmod(shard.shape[0], LANES)
            held[self.own + (slice(0, full), slice(None))] = shard[0 : full * LANES].reshape(full, LANES)
            if rest:
                held[self.own + (slice(full, full + 1), slice(0, rest))] = shard[full * LANES :].reshape(1, rest)
        for block in BLOCKS:
            self.s.blocks[block.index].sums[...] = jnp.zeros((8, plan.width), F32)
        self.norm_columns()
        self.documents()
        self.wait_entry()
        self.open_gathers()
        self.gather_step()
        self.loaded()
        for s in range(plan.seqs):
            self.act(
                ENCODER,
                OUTER,
                s,
                plan.width,
                lambda rows, t, fresh=False: self.s.given[rows, self.lanes_of(s, t)].astype(F32),
            )
            self.gather_step()
        self.forward()
        for gather in self.gathers:
            gather.leave()
        self.loaded()
        total, given, dq = self.s.total, self.s.given, self.s.blocks[1].acts[OUTER].value

        def finish_dec(s, rows, t, back):
            lanes = self.lanes_of(s, t)
            value = given[rows, lanes].astype(F32) + back
            total[rows, lanes] = value
            dq[rows, lanes] = value.astype(BF16)

        def finish_enc(s, rows, t, back):
            lanes = self.lanes_of(s, t)
            total[rows, lanes] = total[rows, lanes] + back

        self.backward(DECODER, given, finish_dec, lambda s: None)
        self.load(self.ins.tokens)
        stores = []

        def done_enc(s):
            copy = pltpu.make_async_copy(
                total.at[:, self.lanes_of(s)], self.outs.grad_tokens.at[s], self.s.local_sem.at[8 + s]
            )
            copy.start()
            stores.append(copy)

        self.backward(ENCODER, dq, finish_enc, done_enc, self.loaded)
        while self.in_flight:
            self.tick()
        for item in self.scatters + self.reduces:
            item.leave()
        for copy in stores + [self.storing]:
            copy.wait()
        for block, item in zip((DECODER, ENCODER), self.reduces):
            base = plan.small_at[6 + block.index]
            for tile in range(plan.norm_tiles):
                begin, size = tile_span(tile, plan.width)
                self.outs.small[base + 8 * tile : base + 8 * tile + 8, 0:size] = item.result[:, begin : begin + size]


def per_device(
    grid,
    tokens,
    cotangent,
    doc_starts,
    enc_first,
    enc_conv,
    enc_last,
    enc_norm_first,
    enc_norm_inner,
    dec_first,
    dec_conv,
    dec_last,
    dec_norm_first,
    dec_norm_inner,
):
    seqs, seg, width = tokens.shape
    weights = (enc_first, enc_conv, enc_last, dec_first, dec_conv, dec_last)
    norms = [enc_norm_first, enc_norm_inner, dec_norm_first, dec_norm_inner]
    plan = Plan(grid, seqs, seg, width, [w.shape[0] for w in weights])
    vmem = pl.BlockSpec(memory_space=pltpu.VMEM)
    hbm = pl.BlockSpec(memory_space=pl.ANY)
    smem = pl.BlockSpec(memory_space=pltpu.SMEM)
    ins = dict(
        doc_starts=doc_starts,
        tokens=jnp.swapaxes(tokens, 1, 2),
        cotangent=jnp.swapaxes(cotangent, 1, 2),
        shards=list(weights),
        norms=norms,
    )
    in_specs = dict(doc_starts=smem, tokens=hbm, cotangent=hbm, shards=[vmem] * 6, norms=[vmem] * 4)
    shape = jax.ShapeDtypeStruct
    outs = dict(
        out=shape((seqs, width, seg), BF16),
        grad_tokens=shape((seqs, width, seg), F32),
        small=shape((plan.small_at[-1], LANES), F32),
    )
    out_specs = dict(out=hbm, grad_tokens=hbm, small=vmem)
    trees = [jax.tree.structure(tree) for tree in (ins, outs, plan.scratch)]

    def body(*refs):
        named = []
        for tree in trees:
            named.append(spaces(jax.tree.unflatten(tree, refs[: tree.num_leaves])))
            refs = refs[tree.num_leaves :]
        Kernel(plan, *named).run()

    results = pl.pallas_call(
        body,
        out_shape=jax.tree.leaves(outs),
        in_specs=jax.tree.leaves(in_specs),
        out_specs=jax.tree.leaves(out_specs),
        scratch_shapes=jax.tree.leaves(plan.scratch),
        compiler_params=pltpu.CompilerParams(
            collective_id=0, has_side_effects=True, vmem_limit_bytes=64 * 1024 * 1024 - 65536
        ),
    )(*jax.tree.leaves(ins))
    result = spaces(jax.tree.unflatten(trees[1], results))
    parts = hand_over(plan, result.small, weights, norms)
    out, grad_tokens = jnp.swapaxes(result.out, 1, 2), jnp.swapaxes(result.grad_tokens, 1, 2)
    return (out, grad_tokens, *parts[:3], *parts[6:8], *parts[3:6], *parts[8:])


def hand_over(plan, small, weights, norms):
    def body(small, *outs):
        for out, begin in zip(outs[:6], plan.small_at):
            full, rest = divmod(out.shape[0], LANES)
            out[0 : full * LANES] = small[begin : begin + full].reshape(full * LANES)
            if rest:
                out[full * LANES :] = small[begin + full, 0:rest]
        for k, out in enumerate(outs[6:]):
            begin = plan.small_at[6 + k // 2] + 2 * (k % 2)
            count, width = out.shape
            for tile in range(-(-width // LANES)):
                low, size = tile_span(tile, width)
                out[:, low : low + size] = small[begin + 8 * tile : begin + 8 * tile + count, 0:size]

    return pl.pallas_call(
        body, out_shape=[jax.ShapeDtypeStruct(value.shape, F32) for value in (*weights, *norms)]
    )(small)


def solution(mesh):
    flat = P(("batch", "seq"))
    rows = P("batch", "seq", None)
    in_specs = (rows, rows, P("batch", None), flat, flat, flat, P(), P(), flat, flat, flat, P(), P())
    out_specs = (rows, rows, flat, flat, flat, P(), P(), flat, flat, flat, P(), P())
    return jax.shard_map(
        functools.partial(per_device, Grid(mesh)),
        mesh=mesh,
        in_specs=in_specs,
        out_specs=out_specs,
        check_vma=False,
    )
```

```python
import functools
import types

import jax
import jax.numpy as jnp
from jax import lax
from jax.experimental import pallas as pl
from jax.experimental.pallas import tpu as pltpu
from jax.sharding import PartitionSpec as P

H = 400
ENCODER_TAPS = 5
ENCODER_DILATION = 4
DECODER_TAPS = 3
DECODER_DILATION = 16

F32, BF16 = jnp.float32, jnp.bfloat16
MESH = pl.DeviceIdType.MESH
LANES = 128
TILES = 4
CHUNK = 16
REACH = 32
SHARE = 112
SLACK = 8
EPS = 1e-5
HI, LO, CORE, SEQ = 0, 1, 2, 3
ORDER_A = (HI, LO, SEQ, CORE)
ORDER_C = (SEQ, HI, LO, CORE)
LAG = 1
PACE = 3.0
UNROLL = 12
STEP, STEP_UNROLL = 80, 4


def round_up(value, step):
    return -(-value // step) * step


class Grid:
    def __init__(self, mesh):
        batch, seq = mesh.shape["batch"], mesh.shape["seq"]
        lo = 2 if batch <= 16 else 4
        self.sizes = (batch // (2 * lo), lo, 2, seq)
        self.count = batch * seq

    def own(self):
        batch = lax.axis_index("batch")
        lo = self.sizes[1]
        return (batch // (2 * lo), (batch // 2) % lo, batch % 2, lax.axis_index("seq"))

    def device(self, place):
        hi, lo, core, seq = place
        return ((hi * self.sizes[1] + lo) * 2 + core, seq)

    def peer(self, own, dim, distance):
        place = list(own)
        place[dim] = lax.rem(own[dim] + distance, self.sizes[dim])
        return tuple(place)

    def slot(self, dim, distance):
        return sum(size - 1 for size in self.sizes[:dim]) + distance - 1

    def slots(self):
        return sum(size - 1 for size in self.sizes)


def split_rows(rows):
    first = round_up(int(rows * 0.6), 16)
    parts = [(0, first, ORDER_A)]
    if first < rows:
        parts.append((first, rows - first, ORDER_C))
    return parts


def remote(source, target, send, receive, device):
    copy = pltpu.make_async_remote_copy(
        source, target, send, receive, device_id=device, device_id_type=MESH
    )
    copy.start()
    return copy


class Gather:
    def __init__(self, grid, own, held, send, receive, rows):
        self.grid, self.own, self.held = grid, own, held
        self.send, self.receive = send, receive
        self.parts = split_rows(rows)
        self.copies = {}

    def start(self, stage):
        for color, (begin, count, order) in enumerate(self.parts):
            dim, done = order[stage], order[:stage]
            index = tuple(slice(None) if d in done else self.own[d] for d in range(4))
            block = self.held.at[index + (pl.ds(begin, count),)]
            copies = []
            for distance in range(1, self.grid.sizes[dim]):
                slot = self.grid.slot(dim, distance)
                target = self.grid.device(self.grid.peer(self.own, dim, distance))
                copies.append(
                    remote(
                        block,
                        block,
                        self.send.at[color, slot],
                        self.receive.at[color, slot],
                        target,
                    )
                )
            self.copies[color, stage] = copies

    def arrive(self, stage):
        for color in range(len(self.parts)):
            for copy in self.copies[color, stage]:
                copy.wait_recv()

    def leave(self):
        for copies in self.copies.values():
            for copy in copies:
                copy.wait_send()


def landing_shapes(grid, rows):
    shapes = []
    for begin, count, order in split_rows(rows):
        back = order[::-1]
        for stage, dim in enumerate(back):
            rest = tuple(grid.sizes[d] for d in range(4) if d not in back[: stage + 1])
            shapes.append((grid.sizes[dim] - 1,) + rest + (count, LANES))
    return shapes


class Scatter:
    def __init__(self, grid, own, held, landing, send, receive, rows, result):
        self.grid, self.own, self.held, self.landing = grid, own, held, landing
        self.send, self.receive, self.result = send, receive, result
        self.parts = split_rows(rows)
        self.copies = {}
        self.stage = 0

    def start(self):
        for color, (begin, count, order) in enumerate(self.parts):
            back = order[::-1]
            dim, done = back[self.stage], back[: self.stage]
            copies = []
            for distance in range(1, self.grid.sizes[dim]):
                place = self.grid.peer(self.own, dim, distance)
                index = tuple(
                    self.own[d] if d in done else place[d] if d == dim else slice(None)
                    for d in range(4)
                )
                slot = self.grid.slot(dim, distance)
                copies.append(
                    remote(
                        self.held.at[index + (pl.ds(begin, count),)],
                        self.landing[color * 4 + self.stage].at[distance - 1],
                        self.send.at[color, slot],
                        self.receive.at[color, slot],
                        self.grid.device(place),
                    )
                )
            self.copies[color, self.stage] = copies

    def finish(self):
        for color, (begin, count, order) in enumerate(self.parts):
            back = order[::-1]
            done = back[: self.stage + 1]
            rest = [d for d in range(4) if d not in done]
            for copy in self.copies[color, self.stage]:
                copy.wait_recv()
            landing = self.landing[color * 4 + self.stage]
            senders = landing.shape[0]
            blocks = 1
            for d in rest:
                blocks *= self.grid.sizes[d]

            def add(block, carry, begin=begin, count=count, landing=landing, rest=rest):
                left, place = block, {}
                for d in reversed(rest):
                    place[d] = left % self.grid.sizes[d]
                    left = left // self.grid.sizes[d]
                index = tuple(place.get(d, self.own[d]) for d in range(4))
                total = self.held[index + (pl.ds(begin, count),)].astype(F32)
                for sender in range(senders):
                    where = (sender,) + tuple(place[d] for d in rest)
                    total = total + landing[where].astype(F32)
                if rest:
                    self.held[index + (pl.ds(begin, count),)] = total.astype(BF16)
                else:
                    self.result[pl.ds(begin, count), :] = total
                return carry

            if blocks == 1:
                add(0, 0)
            else:
                lax.fori_loop(0, blocks, add, 0, unroll=2 if blocks % 2 == 0 else 1)
        self.stage += 1

    def leave(self):
        for copies in self.copies.values():
            for copy in copies:
                copy.wait_send()


class Reduce:
    ORDER = (CORE, SEQ, LO, HI)

    def __init__(self, grid, own, slots, send, receive):
        self.grid, self.own, self.slots = grid, own, slots
        self.send, self.receive = send, receive
        self.copies = {}
        self.stage = 0

    def start(self, value=None):
        dim = self.ORDER[self.stage]
        slots, mine = self.slots[dim], self.own[dim]
        if value is not None:
            slots[mine] = value
        self.copies[self.stage] = [
            remote(
                slots.at[mine],
                slots.at[mine],
                self.send.at[self.grid.slot(dim, distance)],
                self.receive.at[self.grid.slot(dim, distance)],
                self.grid.device(self.grid.peer(self.own, dim, distance)),
            )
            for distance in range(1, self.grid.sizes[dim])
        ]

    def finish(self):
        dim = self.ORDER[self.stage]
        for copy in self.copies[self.stage]:
            copy.wait_recv()
        total = self.slots[dim][0]
        for other in range(1, self.grid.sizes[dim]):
            total = total + self.slots[dim][other]
        self.stage += 1
        if self.stage < 4:
            following = self.ORDER[self.stage]
            self.slots[following][self.own[following]] = total
        else:
            self.result = total

    def leave(self):
        for copies in self.copies.values():
            for copy in copies:
                copy.wait_send()


def lane_ids(rows):
    return lax.broadcasted_iota(jnp.int32, (rows, LANES), 1)


def period_of(elements):
    group = 1
    while (group * elements) % H:
        group *= 2
    return group


class Pieces:
    def __init__(self, grid, elements):
        self.grid, self.elements = grid, elements
        self.rows = round_up(-(-elements // LANES), 16)
        self.pitch = self.rows + SLACK
        self.group = period_of(elements)
        self.groups = grid.count // self.group
        self.period = self.group * elements // H
        self.passes = 2 if self.groups % 16 == 0 else 1
        self.matrix_rows = grid.count * elements // H
        self.part_rows = self.matrix_rows // self.passes

    def flat_rows(self):
        return self.grid.count // self.passes * self.pitch + SLACK

    def each(self, held, flat, part, widen):
        _, lo, core, seq = self.grid.sizes
        count = self.grid.count // self.passes

        def body(local, carry):
            piece = local + part * count
            index = (piece // (lo * core * seq), (piece // (core * seq)) % lo, (piece // seq) % core, piece % seq)
            begin = pl.multiple_of(local * self.pitch + SLACK, SLACK)
            if widen:
                flat[pl.ds(begin, self.rows), :] = held[index].astype(F32)
            else:
                held[index] = flat[pl.ds(begin, self.rows), :].astype(BF16)
            return carry

        lax.fori_loop(0, count, body, 0, unroll=4)

    def at(self, piece, row):
        count = self.groups // self.passes
        return (pl.ds(piece * self.pitch + row, count, stride=self.group * self.pitch), slice(None))

    def row_at(self, row, lead=0):
        count = self.groups // self.passes
        return (pl.ds(row + lead, count, stride=self.period), slice(None))

    def unpack(self, held, flat, matrix, part, lead):
        lane = lane_ids(self.groups // self.passes)
        self.each(held, flat, part, True)
        for piece in range(self.group):
            offset = piece * self.elements
            first, last = -(-offset // H), (offset + self.elements) // H

            def body(row, carry, piece=piece, offset=offset):
                local = row * H - offset + SLACK * LANES
                source, shift = local // LANES, local % LANES
                keep = lane < LANES - shift
                back = lax.rem(LANES - shift, LANES)
                rolled = [
                    pltpu.roll(flat[self.at(piece, source + t)], back, axis=1)
                    for t in range(TILES + 1)
                ]
                for tile in range(TILES):
                    matrix.at[tile][self.row_at(row, lead)] = jnp.where(
                        keep, rolled[tile], rolled[tile + 1]
                    )
                return carry

            if last > first:
                lax.fori_loop(first, last, body, 0, unroll=last - first)
            if (offset + self.elements) % H:
                self.shared_row(flat, matrix, piece, last, lane, lead)

    def shared_row(self, flat, matrix, piece, row, lane, lead):
        local = row * H - piece * self.elements
        cut = (piece + 1) * self.elements - row * H
        for tile in range(TILES):
            begin, end = tile * LANES, min((tile + 1) * LANES, H)
            value = jnp.zeros(lane.shape, F32)
            position = begin
            while position < end:
                if position < cut:
                    owner, at, stop = piece, local + position, min(end, cut)
                else:
                    owner, at, stop = piece + 1, position - cut, end
                source, slot = at // LANES + SLACK, at % LANES
                stop = min(stop, position + LANES - slot)
                goal = position - begin
                rolled = pltpu.roll(flat[self.at(owner, source)], (goal - slot) % LANES, axis=1)
                value = jnp.where((lane >= goal) & (lane < goal + stop - position), rolled, value)
                position = stop
            matrix.at[tile][self.row_at(row, lead)] = value

    def pack(self, matrix, flat, held, part):
        lane = lane_ids(self.groups // self.passes)
        for piece in range(self.group):
            offset = piece * self.elements
            first, last = offset // H, -(-(offset + self.elements) // H)

            def body(row, pending, piece=piece, offset=offset):
                local = row * H - offset + SLACK * LANES
                target, shift = local // LANES, local % LANES
                keep = lane >= shift
                rolled = [
                    pltpu.roll(matrix.at[tile][self.row_at(row)], shift, axis=1) for tile in range(TILES)
                ]
                before = pending
                for tile in range(TILES):
                    value = jnp.where(keep, rolled[tile], before)
                    flat[self.at(piece, target + tile)] = value
                    before = rolled[tile]
                return jnp.where(shift + H % LANES > LANES, rolled[-1], value)

            pending = lax.fori_loop(first, last, body, jnp.zeros(lane.shape, F32), unroll=last - first)
            ending = (last * H - offset + SLACK * LANES) // LANES
            flat[self.at(piece, ending)] = pending
        self.each(held, flat, part, False)


def dot(a, b, left, right, precision=None):
    return lax.dot_general(
        a, b, (((left,), (right,)), ((), ())), precision=precision, preferred_element_type=F32
    )


def nn(a, b):
    return dot(a, b, 1, 0)


def nt(a, b):
    return dot(a, b, 1, 1)


def tn(a, b):
    return dot(a, b, 0, 0)


def tile_span(tile, width):
    return tile * LANES, min(LANES, width - tile * LANES)


def chunks(count, body, carry=0):
    def step(index, carry):
        return body(pl.multiple_of(index * CHUNK, CHUNK), carry)

    return lax.fori_loop(0, count // CHUNK, step, carry, unroll=UNROLL)


def steps(count, body, carry=0):
    def step(index, carry):
        return body(pl.multiple_of(index * STEP, CHUNK), carry)

    return lax.fori_loop(0, count // STEP, step, carry, unroll=STEP_UNROLL)


def fold(value):
    total = value[0:CHUNK]
    for begin in range(CHUNK, value.shape[0], CHUNK):
        total = total + value[begin : begin + CHUNK]
    return total


def zeros(tiles):
    return (jnp.zeros((CHUNK, LANES), F32),) * tiles


def column_sums(totals, count):
    return [jnp.sum(total, axis=0, keepdims=True) * (1.0 / count) for total in totals]


def gelu_parts(a):
    bell = jnp.exp(a * a * -0.5)
    t = 1.0 / (1.0 + jnp.abs(a) * (0.3275911 * 0.7071067811865476))
    poly = 1.061405429 * t - 1.453152027
    poly = ((poly * t + 1.421413741) * t - 0.284496736) * t + 0.254829592
    tail = poly * t * bell * 0.5
    phi = jnp.where(a >= 0.0, 1.0 - tail, tail)
    return a * phi, phi + a * bell * 0.3989422804014327


class Block:
    def __init__(self, index, offsets, norms):
        self.index, self.offsets = index, offsets
        self.before, self.after = min(offsets) < 0, max(offsets) > 0
        self.norms = norms


ENCODER = Block(
    0, [(j - ENCODER_TAPS // 2) * ENCODER_DILATION for j in range(ENCODER_TAPS)], (0, 1)
)
DECODER = Block(1, [(j - DECODER_TAPS + 1) * DECODER_DILATION for j in range(DECODER_TAPS)], (2, 3))
BLOCKS = (ENCODER, DECODER)
FIRST, CONV, LAST = 0, 1, 2
OUTER, P_NORM, C_NORM = 0, 1, 2


def spaces(tree):
    if isinstance(tree, dict):
        return types.SimpleNamespace(**{key: spaces(value) for key, value in tree.items()})
    if isinstance(tree, (list, tuple)):
        return [spaces(value) for value in tree]
    return tree


class Plan:
    def __init__(self, grid, seqs, seg, width, elements):
        self.grid, self.seqs, self.seg, self.width = grid, seqs, seg, width
        self.rows = seqs * seg
        self.tiles = seg // LANES
        self.pieces = [Pieces(grid, count) for count in elements]
        self.norm_tiles = -(-width // LANES)
        sizes = [p.rows for p in self.pieces] + [8 * self.norm_tiles] * 2
        self.small_at = [sum(sizes[:k]) for k in range(len(sizes) + 1)]
        vmem, dma = pltpu.VMEM, pltpu.SemaphoreType.DMA
        rows, count = self.rows, len(elements)

        def block(which):
            taps = len(which.offsets)
            half = dict(
                normed=vmem((H, rows), BF16), slope=vmem((H, rows), BF16), value=vmem((H, rows), BF16)
            )
            return dict(
                weights=[vmem((width, H), BF16), vmem((taps * H, H), BF16), vmem((H, width), BF16)],
                acts=[dict(slope=vmem((width, rows), BF16), value=vmem((width, rows), BF16)), half, half],
                halo=[[vmem((2, seqs, SHARE, LANES), BF16) for _ in range(2)] for _ in range(2)],
                stats=vmem((8, rows), F32),
                outer=vmem((2, width, LANES), F32),
                inner=vmem((4, H, LANES), F32),
                sums=vmem((8, width), F32),
                slots=[vmem((size, 8, width), F32) for size in grid.sizes],
            )

        self.scratch = dict(
            held=[vmem(grid.sizes + (p.rows, LANES), BF16) for p in self.pieces],
            landing=[[vmem(shape, BF16) for shape in landing_shapes(grid, p.rows)] for p in self.pieces],
            flat=vmem((max(p.flat_rows() for p in self.pieces), LANES), F32),
            matrix=vmem((TILES, max(p.part_rows for p in self.pieces) + 16, LANES), F32),
            blocks=[block(which) for which in BLOCKS],
            given=vmem((width, rows), BF16),
            total=vmem((width, rows), F32),
            staged=vmem((width, seg), BF16),
            wide=vmem((seqs, H, seg + 2 * LANES), BF16),
            begin=vmem((seqs, CHUNK, seg + 2 * LANES), jnp.int32),
            taps=vmem((ENCODER_TAPS * H, rows), BF16),
            broad=vmem((width, rows), F32),
            spread=vmem((2, width, LANES), F32),
            local_sem=dma((count + 2 * seqs + 2,)),
            gather_sem=dma((2, count, 2, grid.slots())),
            scatter_sem=dma((2, count, 2, grid.slots())),
            reduce_sem=dma((2, 2, grid.slots())),
            halo_sem=dma((2, 4, seqs, 2)),
        )


class Kernel:
    def __init__(self, plan, ins, outs, scratch):
        self.plan, self.grid, self.own = plan, plan.grid, plan.grid.own()
        self.ins, self.outs, self.s = ins, outs, scratch
        self.in_flight, self.scatters, self.reduces = [], [], []
        self.clock = 0.0


    def signal_entry(self):
        barrier = pltpu.get_barrier_semaphore()
        for dim in range(4):
            for distance in range(1, self.grid.sizes[dim]):
                pl.semaphore_signal(
                    barrier,
                    inc=1,
                    device_id=self.grid.device(self.grid.peer(self.own, dim, distance)),
                    device_id_type=MESH,
                )

    def wait_entry(self):
        pl.semaphore_wait(pltpu.get_barrier_semaphore(), self.grid.slots())

    def open_gathers(self):
        self.gathers = [
            Gather(
                self.grid,
                self.own,
                self.s.held[k],
                self.s.gather_sem.at[0, k],
                self.s.gather_sem.at[1, k],
                pieces.rows,
            )
            for k, pieces in enumerate(self.plan.pieces)
        ]
        self.step, self.arrived = 0, set()

    def gather_step(self):
        t, count = self.step, len(self.gathers)
        if t >= count + 4 * LAG:
            return
        for stage in reversed(range(4)):
            k = t - LAG * (stage + 1)
            if 0 <= k < count:
                if stage < 3 or k not in self.arrived:
                    self.gathers[k].arrive(stage)
                if stage < 3:
                    self.gathers[k].start(stage + 1)
        if t < count:
            self.gathers[t].start(0)
        self.step += 1

    def gather_until(self, k):
        while self.step < k + 4 * LAG:
            self.gather_step()
        if k not in self.arrived and self.step == k + 4 * LAG:
            self.gathers[k].arrive(3)
            self.arrived.add(k)

    def tick(self, spent=None):
        self.clock += spent or 0.0
        for item in list(self.in_flight):
            if spent is None or self.clock - item.began >= item.wait[item.stage]:
                item.finish()
                if item.stage < 4:
                    self.begin(item)
                else:
                    self.in_flight.remove(item)

    def begin(self, item, *first):
        item.start(*first)
        item.began = self.clock

    def scatter(self, k):
        item = Scatter(
            self.grid,
            self.own,
            self.s.held[k],
            self.s.landing[k],
            self.s.scatter_sem.at[0, k],
            self.s.scatter_sem.at[1, k],
            self.plan.pieces[k].rows,
            self.outs.small.at[pl.ds(self.plan.small_at[k], self.plan.pieces[k].rows)],
        )
        per_row = self.plan.pieces[k].rows * 0.01
        item.wait = [PACE * (1.5 + per_row)] + [PACE * (3.0 + 2 * per_row)] * 3
        self.begin(item)
        self.in_flight.append(item)
        self.scatters.append(item)

    def reduce(self, block):
        k, refs = block.index, self.s.blocks[block.index]
        item = Reduce(
            self.grid, self.own, refs.slots, self.s.reduce_sem.at[0, k], self.s.reduce_sem.at[1, k]
        )
        item.wait = [1.5, 3.0, 3.0, 3.0]
        self.begin(item, refs.sums[...])
        self.in_flight.append(item)
        self.reduces.append(item)

    def send_halo(self, block, way, s):
        seg, size, way_refs = self.plan.seg, self.grid.sizes[SEQ], self.s.blocks[block.index].halo[way]
        before, after = (block.after, block.before) if way else (block.before, block.after)
        copies = []
        for side, wanted, begin, distance in ((0, before, seg, 1), (1, after, LANES, size - 1)):
            if wanted:
                phase = 2 * block.index + way
                message = way_refs[side].at[0, s]
                self.pack_halo(s, begin, LANES - REACH if side == 0 else 0, message)
                copy = remote(
                    message,
                    way_refs[side].at[1, s],
                    self.s.halo_sem.at[0, phase, s, side],
                    self.s.halo_sem.at[1, phase, s, side],
                    self.grid.device(self.grid.peer(self.own, SEQ, distance)),
                )
                copies.append((side, copy))
        return copies

    def shares(self):
        return [(quarter, begin, min(SHARE, H - begin)) for quarter, begin in enumerate(range(0, H, SHARE))]

    def pack_halo(self, s, begin, lane, message):
        lanes = lane_ids(SHARE)
        total = jnp.zeros((SHARE, LANES), F32)
        for quarter, row, rows in self.shares():
            value = self.s.wide[s, row : row + rows, begin : begin + LANES].astype(F32)
            if rows < SHARE:
                value = jnp.concatenate([value, jnp.zeros((SHARE - rows, LANES), F32)], axis=0)
            value = pltpu.roll(value, (quarter * REACH - lane) % LANES, axis=1)
            total = jnp.where(lanes >= quarter * REACH, value, total)
        message[...] = total.astype(BF16)

    def take_halo(self, block, way, s, copies):
        for side, copy in copies:
            copy.wait()
            begin = (self.plan.seg + LANES) if side else 0
            lane = 0 if side else LANES - REACH
            message = self.s.blocks[block.index].halo[way][side][1, s].astype(F32)
            for quarter, row, rows in self.shares():
                value = pltpu.roll(message, (lane - quarter * REACH) % LANES, axis=1)
                self.s.wide[s, row : row + rows, begin : begin + LANES] = value[0:rows].astype(BF16)


    def unpack(self, k):
        self.gather_until(k)
        pieces, matrix, step = self.plan.pieces[k], self.s.matrix, 32 if k % 3 == LAST else 16
        lead = 0
        for part in range(pieces.passes):
            pieces.unpack(self.s.held[k], self.s.flat, matrix, part, lead)
            ready = (lead + pieces.part_rows) // step * step
            self.convert(k, part * pieces.part_rows - lead, ready)
            lead = lead + pieces.part_rows - ready
            if lead:
                matrix[:, 0:lead, :] = matrix[:, ready : ready + lead, :]

    def convert(self, k, base, rows):
        target = self.s.blocks[k // 3].weights[k % 3]
        matrix, chunk = self.s.matrix, 16
        if k % 3 == LAST:
            keep = lane_ids(chunk) < H % LANES

            def body(index, carry):
                r = pl.multiple_of(index * chunk, 16)
                left = [matrix.at[c][pl.ds(2 * r, chunk, stride=2), :] for c in range(TILES)]
                right = [
                    pltpu.roll(matrix.at[c][pl.ds(2 * r + 1, chunk, stride=2), :], H % LANES, axis=1)
                    for c in range(TILES)
                ]
                tiles = left[:3] + [jnp.where(keep, left[3], right[0])]
                tiles += [jnp.where(keep, right[c], right[c + 1]) for c in range(3)]
                for c, value in enumerate(tiles):
                    begin, size = tile_span(c, target.shape[1])
                    goal = pl.multiple_of(base // 2 + r, 16)
                    target[pl.ds(goal, chunk), begin : begin + size] = value[:, :size].astype(BF16)
                return carry

            lax.fori_loop(0, rows // (2 * chunk), body, 0, unroll=4)
        else:

            def body(index, carry):
                r = pl.multiple_of(index * chunk, 16)
                goal = pl.multiple_of(base + r, 16)
                for c in range(TILES):
                    begin, size = tile_span(c, H)
                    target[pl.ds(goal, chunk), begin : begin + size] = matrix[c, pl.ds(r, chunk), :size].astype(BF16)
                return carry

            lax.fori_loop(0, rows // chunk, body, 0, unroll=4)

    def give(self, k, part):
        pieces = self.plan.pieces[k]
        pieces.pack(self.s.matrix, self.s.flat, self.s.held[k], part)
        if part == pieces.passes - 1:
            self.scatter(k)

    def grad_rows(self, begin, value):
        for c in range(TILES):
            low, size = tile_span(c, H)
            self.s.matrix[c, begin : begin + value.shape[0], 0:size] = value[:, low : low + size]

    def give_rows(self, k, values):
        pieces, broad = self.plan.pieces[k], self.s.broad
        part, room = 0, pieces.part_rows
        for value in values:
            begin = 0
            while begin < H:
                count = min(room, H - begin)
                if begin:
                    self.grad_rows(pieces.part_rows - room, broad[0:count, 0:H])
                else:
                    self.grad_rows(pieces.part_rows - room, value[0:count])
                    if count < H:
                        broad[0 : H - count, 0:H] = value[count:]
                begin, room = begin + count, room - count
                if not room:
                    self.give(k, part)
                    self.tick(1.0)
                    part, room = part + 1, pieces.part_rows
            self.tick(1.0)

    def give_last(self, k, value):
        width, matrix, chunk = self.plan.width, self.s.matrix, 40
        pieces, store = self.plan.pieces[k], self.s.broad
        tiles_of = -(-width // LANES)
        store[0:H, 0:width] = value
        keep = lane_ids(chunk) < LANES - H % LANES
        for part in range(pieces.passes):
            base = part * pieces.part_rows // 2

            def body(index, carry, base=base):
                r = pl.multiple_of(index * chunk, 8)
                rows = pl.ds(pl.multiple_of(base + r, 8), chunk)
                tiles = [store[rows, c * LANES : (c + 1) * LANES] for c in range(tiles_of)]
                for c in range(TILES):
                    matrix.at[c][pl.ds(2 * r, chunk, stride=2), :] = tiles[c]
                back = [pltpu.roll(value, LANES - H % LANES, axis=1) for value in tiles[3:]]
                back.append(back[-1])
                for c in range(TILES):
                    matrix.at[c][pl.ds(2 * r + 1, chunk, stride=2), :] = jnp.where(keep, back[c], back[c + 1])
                return carry

            lax.fori_loop(0, pieces.part_rows // (2 * chunk), body, 0)
            self.give(k, part)


    def documents(self):
        seg, span = self.plan.seg, self.plan.seg + 2 * LANES
        whole = seg * self.grid.sizes[SEQ]
        place = lax.broadcasted_iota(jnp.int32, (CHUNK, span), 1) + (self.own[SEQ] * seg - LANES)
        for s in range(self.plan.seqs):
            begin = jnp.zeros((CHUNK, span), jnp.int32)
            for k in range(self.ins.doc_starts.shape[1]):
                head = self.ins.doc_starts[s, k]
                begin = jnp.maximum(begin, jnp.where(place >= head, head, 0))
            begin = jnp.where(place < 0, -1, begin)
            self.s.begin[s] = jnp.where(place >= whole, -2, begin)

    def shifted(self, tiles, shift, lane):
        count = len(tiles) - 2
        if not shift:
            return tiles[1:-1]
        rolled = [pltpu.roll(tile, -shift % LANES, axis=1) for tile in tiles]
        if shift > 0:
            return [jnp.where(lane < LANES - shift, rolled[c + 1], rolled[c + 2]) for c in range(count)]
        return [jnp.where(lane >= -shift, rolled[c + 1], rolled[c]) for c in range(count)]

    def spread_taps(self, block, s, sign):
        count, seg, wide, taps = self.plan.tiles, self.plan.seg, self.s.wide, self.s.taps
        lane = lane_ids(CHUNK)
        heads = [self.s.begin[s, :, t * LANES : (t + 1) * LANES] for t in range(count + 2)]
        inside = [
            [there == here for there, here in zip(self.shifted(heads, sign * offset, lane), heads[1:-1])]
            for offset in block.offsets
        ]

        def body(r, carry):
            tiles = [wide[s, pl.ds(r, CHUNK), t * LANES : (t + 1) * LANES].astype(F32) for t in range(count + 2)]
            for j, offset in enumerate(block.offsets):
                for t, value in enumerate(self.shifted(tiles, sign * offset, lane)):
                    if offset:
                        value = jnp.where(inside[j][t], value, 0.0)
                    begin = s * seg + t * LANES
                    taps[pl.ds(pl.multiple_of(j * H + r, CHUNK), CHUNK), begin : begin + LANES] = value.astype(BF16)
            return carry

        chunks(H, body)


    def norm_columns(self):
        for block in BLOCKS:
            refs = self.s.blocks[block.index]
            for source, target in zip(block.norms, (refs.outer, refs.inner)):
                rows = self.ins.norms[source]
                for k in range(rows.shape[0]):
                    for tile in range(-(-rows.shape[1] // LANES)):
                        begin, size = tile_span(tile, rows.shape[1])
                        row = rows[k : k + 1, begin : begin + size]
                        target[k, begin : begin + size, :] = jnp.broadcast_to(row, (LANES, size)).T

    def gains(self, block, norm):
        refs = self.s.blocks[block.index]
        if norm == OUTER:
            return refs.outer.at[0], refs.outer.at[1]
        return refs.inner.at[2 * norm - 2], refs.inner.at[2 * norm - 1]

    def lanes_of(self, s, t=None):
        if t is None:
            return slice(s * self.plan.seg, (s + 1) * self.plan.seg)
        begin = s * self.plan.seg + t * LANES
        return slice(begin, begin + LANES)

    def act(self, block, norm, s, count, load, wide=False):
        tiles = range(self.plan.tiles)
        refs = self.s.blocks[block.index]
        act, stats = refs.acts[norm], refs.stats
        gain, shift = self.gains(block, norm)

        def first(r, carry):
            rows = pl.ds(r, STEP)
            return tuple(carry[t] + fold(load(rows, t, True)) for t in tiles)

        centre = column_sums(steps(count, first, zeros(len(tiles))), count)

        def second(r, carry):
            rows, out = pl.ds(r, STEP), []
            for t in tiles:
                away = load(rows, t) - centre[t]
                out.append(carry[t] + fold(away * away))
            return tuple(out)

        spread = column_sums(steps(count, second, zeros(len(tiles))), count)
        scale = [lax.rsqrt(value + EPS) for value in spread]

        def third(r, carry):
            rows = pl.ds(r, STEP)
            g, b = gain[rows, :], shift[rows, :]
            for t in tiles:
                lanes = self.lanes_of(s, t)
                normed = (load(rows, t) - centre[t]) * scale[t]
                value, slope = gelu_parts(normed * g + b)
                value = value.astype(BF16)
                act.value[rows, lanes] = value
                act.slope[rows, lanes] = slope.astype(BF16)
                if norm != OUTER:
                    act.normed[rows, lanes] = normed.astype(BF16)
                if wide:
                    self.s.wide[s, rows, (t + 1) * LANES : (t + 2) * LANES] = value
            return carry

        steps(count, third)
        for t in tiles:
            lanes = self.lanes_of(s, t)
            if norm == OUTER:
                stats[0:1, lanes] = centre[t]
            stats[norm + 1 : norm + 2, lanes] = scale[t]

    def act_back(self, block, norm, s, count, store, broad):
        tiles = range(self.plan.tiles)
        refs, spread = self.s.blocks[block.index], self.s.spread
        act, stats = refs.acts[norm], refs.stats
        gain, _ = self.gains(block, norm)
        scale = [stats[norm + 1 : norm + 2, self.lanes_of(s, t)] for t in tiles]
        centre = [stats[0:1, self.lanes_of(s, t)] for t in tiles]

        def normed(rows, t):
            if norm == OUTER:
                return (self.x_in(block, rows, self.lanes_of(s, t)) - centre[t]) * scale[t]
            return act.normed[rows, self.lanes_of(s, t)].astype(F32)

        def first(r, carry):
            rows = pl.ds(r, STEP)
            g = gain[rows, :]
            ones, twos = [], []
            for t in tiles:
                e = broad[rows, self.lanes_of(s, t)] * act.slope[rows, self.lanes_of(s, t)].astype(F32)
                n = normed(rows, t)
                en, weighted = e * n, e * g
                ones.append(carry[0][t] + fold(weighted))
                twos.append(carry[1][t] + fold(weighted * n))
                gains, shifts = (gains + en, shifts + e) if t else (en, e)
            if s:
                gains, shifts = gains + spread[0, rows, :], shifts + spread[1, rows, :]
            spread[0, rows, :] = gains
            spread[1, rows, :] = shifts
            return tuple(ones), tuple(twos)

        ones, twos = steps(count, first, (zeros(len(tiles)), zeros(len(tiles))))
        ones, twos = column_sums(ones, count), column_sums(twos, count)

        def second(r, carry):
            rows = pl.ds(r, STEP)
            g = gain[rows, :]
            for t in tiles:
                lanes = self.lanes_of(s, t)
                weighted = broad[rows, lanes] * act.slope[rows, lanes].astype(F32) * g
                store(rows, t, (weighted - ones[t] - normed(rows, t) * twos[t]) * scale[t])
            return carry

        return lambda: steps(count, second)

    def norm_grads(self, block, norm, count):
        sums = self.s.blocks[block.index].sums
        for k in range(2):
            for tile in range(-(-count // LANES)):
                begin, size = tile_span(tile, count)
                block_rows = self.s.spread[k, begin : begin + size, :].T
                sums[2 * norm + k : 2 * norm + k + 1, begin : begin + size] = jnp.sum(
                    block_rows, axis=0, keepdims=True
                )


    def from_broad(self, s):
        return lambda rows, t, again=False: self.s.broad[rows, self.lanes_of(s, t)]

    def forward_inner(self, block):
        refs, broad = self.s.blocks[block.index], self.s.broad
        base, taps = 3 * block.index, len(block.offsets)
        seqs = range(self.plan.seqs)
        self.unpack(base + FIRST)
        halos = []
        broad[0:H, :] = tn(refs.weights[FIRST][...], refs.acts[OUTER].value[...])
        self.gather_step()
        for s in seqs:
            self.act(block, P_NORM, s, H, self.from_broad(s), wide=True)
            halos.append(self.send_halo(block, 0, s))
        self.unpack(base + CONV)
        for s in seqs:
            self.take_halo(block, 0, s, halos[s])
            self.spread_taps(block, s, 1)
        broad[0:H, :] = tn(refs.weights[CONV][...], self.s.taps[0 : taps * H, :])
        self.gather_step()
        for s in seqs:
            self.act(block, C_NORM, s, H, self.from_broad(s))
        self.unpack(base + LAST)

    def forward(self):
        broad, total, plan = self.s.broad, self.s.total, self.plan
        self.forward_inner(ENCODER)
        refs = self.s.blocks[0]
        broad[...] = tn(refs.weights[LAST][...], refs.acts[C_NORM].value[...])
        self.gather_step()
        for s in range(plan.seqs):

            def load(rows, t, fresh=False, s=s):
                lanes = self.lanes_of(s, t)
                if fresh:
                    total[rows, lanes] = self.s.given[rows, lanes].astype(F32) + broad[rows, lanes]
                return total[rows, lanes]

            self.act(DECODER, OUTER, s, plan.width, load)
        self.load(self.ins.cotangent)
        self.forward_inner(DECODER)
        refs = self.s.blocks[1]
        broad[...] = tn(refs.weights[LAST][...], refs.acts[C_NORM].value[...])
        self.gather_step()
        for s in range(plan.seqs):
            if s:
                copy.wait()

            def finish(r, carry, s=s):
                rows = pl.ds(r, CHUNK)
                value = total[rows, self.lanes_of(s)] + broad[rows, self.lanes_of(s)]
                self.s.staged[rows, :] = value.astype(BF16)
                return carry

            chunks(plan.width, finish)
            copy = pltpu.make_async_copy(self.s.staged, self.outs.out.at[s], self.s.local_sem.at[6])
            copy.start()
        self.storing = copy


    def backward(self, block, dq, finish, done, ready=None):
        refs, broad, taps = self.s.blocks[block.index], self.s.broad, self.s.taps
        base, seqs = 3 * block.index, range(self.plan.seqs)
        v, w, u = (refs.acts[k].value for k in (P_NORM, C_NORM, OUTER))
        halos = []
        broad[0:H, :] = nn(refs.weights[LAST][...], dq[...])
        for s in seqs:

            def store(rows, t, value, s=s):
                self.s.wide[s, rows, (t + 1) * LANES : (t + 2) * LANES] = value.astype(BF16)

            self.act_back(block, C_NORM, s, H, store, broad)()
            halos.append(self.send_halo(block, 1, s))
            self.tick(1.5)
        self.norm_grads(block, C_NORM, H)
        self.give_last(base + LAST, nt(w[...], dq[...]))
        self.tick(3.0)
        for s in seqs:
            self.take_halo(block, 1, s, halos[s])
            self.spread_taps(block, s, -1)
            self.tick(1.0)
        self.give_rows(
            base + CONV, (nt(v[...], taps[j * H : (j + 1) * H, :]) for j in range(len(block.offsets)))
        )
        for j in range(len(block.offsets)):
            part = nn(refs.weights[CONV][j * H : (j + 1) * H, :], taps[j * H : (j + 1) * H, :])
            broad[0:H, :] = broad[0:H, :] + part if j else part
            self.tick(1.0)
        for s in seqs:

            def store(rows, t, value, s=s):
                v[rows, self.lanes_of(s, t)] = value.astype(BF16)

            self.act_back(block, P_NORM, s, H, store, broad)()
            self.tick(1.0)
        self.norm_grads(block, P_NORM, H)
        value = nt(u[...], v[...])
        self.give_rows(base + FIRST, [value[0:H], value[H : 2 * H]])
        self.tick(1.5)
        if ready is not None:
            ready()
        rest = []
        broad[...] = nn(refs.weights[FIRST][...], v[...])
        self.tick(1.2)
        for s in seqs:
            store = functools.partial(finish, s)
            rest.append(self.act_back(block, OUTER, s, self.plan.width, store, broad))
            self.tick(1.0)
        self.norm_grads(block, OUTER, self.plan.width)
        self.reduce(block)
        for s in seqs:
            rest[s]()
            done(s)
            self.tick(1.0)

    def x_in(self, block, rows, lanes):
        if block is ENCODER:
            return self.s.given[rows, lanes].astype(F32)
        return self.s.total[rows, lanes]

    def load(self, source):
        self.loading = [
            pltpu.make_async_copy(source.at[s], self.s.given.at[:, self.lanes_of(s)], self.s.local_sem.at[8 + s])
            for s in range(self.plan.seqs)
        ]
        for copy in self.loading:
            copy.start()

    def loaded(self):
        for copy in self.loading:
            copy.wait()

    def run(self):
        plan = self.plan
        self.signal_entry()
        self.load(self.ins.tokens)
        for shard, held in zip(self.ins.shards, self.s.held):
            full, rest = divmod(shard.shape[0], LANES)
            held[self.own + (slice(0, full), slice(None))] = shard[0 : full * LANES].reshape(full, LANES)
            if rest:
                held[self.own + (slice(full, full + 1), slice(0, rest))] = shard[full * LANES :].reshape(1, rest)
        for block in BLOCKS:
            self.s.blocks[block.index].sums[...] = jnp.zeros((8, plan.width), F32)
        self.norm_columns()
        self.documents()
        self.wait_entry()
        self.open_gathers()
        self.gather_step()
        self.loaded()
        for s in range(plan.seqs):
            self.act(
                ENCODER,
                OUTER,
                s,
                plan.width,
                lambda rows, t, fresh=False: self.s.given[rows, self.lanes_of(s, t)].astype(F32),
            )
            self.gather_step()
        self.forward()
        for gather in self.gathers:
            gather.leave()
        self.loaded()
        total, given, dq = self.s.total, self.s.given, self.s.blocks[1].acts[OUTER].value

        def finish_dec(s, rows, t, back):
            lanes = self.lanes_of(s, t)
            value = given[rows, lanes].astype(F32) + back
            total[rows, lanes] = value
            dq[rows, lanes] = value.astype(BF16)

        def finish_enc(s, rows, t, back):
            lanes = self.lanes_of(s, t)
            total[rows, lanes] = total[rows, lanes] + back

        self.backward(DECODER, given, finish_dec, lambda s: None)
        self.load(self.ins.tokens)
        stores = []

        def done_enc(s):
            copy = pltpu.make_async_copy(
                total.at[:, self.lanes_of(s)], self.outs.grad_tokens.at[s], self.s.local_sem.at[8 + s]
            )
            copy.start()
            stores.append(copy)

        self.backward(ENCODER, dq, finish_enc, done_enc, self.loaded)
        while self.in_flight:
            self.tick()
        for item in self.scatters + self.reduces:
            item.leave()
        for copy in stores + [self.storing]:
            copy.wait()
        for block, item in zip((DECODER, ENCODER), self.reduces):
            base = plan.small_at[6 + block.index]
            for tile in range(plan.norm_tiles):
                begin, size = tile_span(tile, plan.width)
                self.outs.small[base + 8 * tile : base + 8 * tile + 8, 0:size] = item.result[:, begin : begin + size]


def per_device(
    grid,
    tokens,
    cotangent,
    doc_starts,
    enc_first,
    enc_conv,
    enc_last,
    enc_norm_first,
    enc_norm_inner,
    dec_first,
    dec_conv,
    dec_last,
    dec_norm_first,
    dec_norm_inner,
):
    seqs, seg, width = tokens.shape
    weights = (enc_first, enc_conv, enc_last, dec_first, dec_conv, dec_last)
    norms = [enc_norm_first, enc_norm_inner, dec_norm_first, dec_norm_inner]
    plan = Plan(grid, seqs, seg, width, [w.shape[0] for w in weights])
    vmem = pl.BlockSpec(memory_space=pltpu.VMEM)
    hbm = pl.BlockSpec(memory_space=pl.ANY)
    smem = pl.BlockSpec(memory_space=pltpu.SMEM)
    ins = dict(
        doc_starts=doc_starts,
        tokens=jnp.swapaxes(tokens, 1, 2),
        cotangent=jnp.swapaxes(cotangent, 1, 2),
        shards=list(weights),
        norms=norms,
    )
    in_specs = dict(doc_starts=smem, tokens=hbm, cotangent=hbm, shards=[vmem] * 6, norms=[vmem] * 4)
    shape = jax.ShapeDtypeStruct
    outs = dict(
        out=shape((seqs, width, seg), BF16),
        grad_tokens=shape((seqs, width, seg), F32),
        small=shape((plan.small_at[-1], LANES), F32),
    )
    out_specs = dict(out=hbm, grad_tokens=hbm, small=vmem)
    trees = [jax.tree.structure(tree) for tree in (ins, outs, plan.scratch)]

    def body(*refs):
        named = []
        for tree in trees:
            named.append(spaces(jax.tree.unflatten(tree, refs[: tree.num_leaves])))
            refs = refs[tree.num_leaves :]
        Kernel(plan, *named).run()

    results = pl.pallas_call(
        body,
        out_shape=jax.tree.leaves(outs),
        in_specs=jax.tree.leaves(in_specs),
        out_specs=jax.tree.leaves(out_specs),
        scratch_shapes=jax.tree.leaves(plan.scratch),
        compiler_params=pltpu.CompilerParams(
            collective_id=0, has_side_effects=True, vmem_limit_bytes=64 * 1024 * 1024 - 65536
        ),
    )(*jax.tree.leaves(ins))
    result = spaces(jax.tree.unflatten(trees[1], results))
    parts = hand_over(plan, result.small, weights, norms)
    out, grad_tokens = jnp.swapaxes(result.out, 1, 2), jnp.swapaxes(result.grad_tokens, 1, 2)
    return (out, grad_tokens, *parts[:3], *parts[6:8], *parts[3:6], *parts[8:])


def hand_over(plan, small, weights, norms):
    def body(small, *outs):
        for out, begin in zip(outs[:6], plan.small_at):
            full, rest = divmod(out.shape[0], LANES)
            out[0 : full * LANES] = small[begin : begin + full].reshape(full * LANES)
            if rest:
                out[full * LANES :] = small[begin + full, 0:rest]
        for k, out in enumerate(outs[6:]):
            begin = plan.small_at[6 + k // 2] + 2 * (k % 2)
            count, width = out.shape
            for tile in range(-(-width // LANES)):
                low, size = tile_span(tile, width)
                out[:, low : low + size] = small[begin + 8 * tile : begin + 8 * tile + count, 0:size]

    return pl.pallas_call(
        body, out_shape=[jax.ShapeDtypeStruct(value.shape, F32) for value in (*weights, *norms)]
    )(small)


def solution(mesh):
    flat = P(("batch", "seq"))
    rows = P("batch", "seq", None)
    in_specs = (rows, rows, P("batch", None), flat, flat, flat, P(), P(), flat, flat, flat, P(), P())
    out_specs = (rows, rows, flat, flat, flat, P(), P(), flat, flat, flat, P(), P())
    return jax.shard_map(
        functools.partial(per_device, Grid(mesh)),
        mesh=mesh,
        in_specs=in_specs,
        out_specs=out_specs,
        check_vma=False,
    )
```
